256 devices in a mesh: tok: 64 (over x, z, core), head: 4 (over y).
Axes of the slice: x: 4, y: 4, z: 8, core: 2. Of those that a mesh axis runs over, the one named last changes fastest.
Arguments:
- queries: bfloat16 [2, 8192, 2048], P(None, 'tok', 'head'), may hold values from -16 to 16
- keys: bfloat16 [8192, 2048], P('tok', 'head'), may hold values from -16 to 16
- values: bfloat16 [8192, 2048], P('tok', 'head'), may hold values from -6 to 6
- upstream: bfloat16 [2, 8192, 2048], P(None, 'tok', 'head'), may hold values from -6 to 6
- out_gain: float32 [2048], P('head'), may hold values from 0.5 to 2
- gate_weight: bfloat16 [4, 512, 512], P('head', 'tok'), may hold values from -0.25 to 0.25
- up_weight: bfloat16 [4, 512, 512], P('head', 'tok'), may hold values from -0.25 to 0.25
- down_weight: bfloat16 [4, 512, 512], P('head', 'tok'), may hold values from -0.25 to 0.25
Outputs:
- grad_queries: bfloat16 [2, 8192, 2048], P(None, 'tok', 'head')
- grad_keys: bfloat16 [8192, 2048], P('tok', 'head')
- grad_values: bfloat16 [8192, 2048], P('tok', 'head')
- grad_gate: float32 [4, 512, 512], P('head', 'tok')
- grad_up: float32 [4, 512, 512], P('head', 'tok')
- grad_down: float32 [4, 512, 512], P('head', 'tok')
The draws below stay inside these ranges and needn't reach their ends.
All inputs are finite; a program needn't handle non-finite values.
Results may differ from the reference program's by a relative error of at most 0.02.
Values may be sent and summed in bfloat16 or wider, within the bound.
A program may use at most 128 MiB of HBM per device.

```python
import math
import jax
import jax.numpy as jnp
from jax import lax

D = 512
H = 512
NS_STEPS = 2
HEADS = 4
BLOCK = 8192


def strengthened(values, rng, source, target, blocks, factor):
    owner, partner = [(jnp.arange(values.shape[dim]) // (values.shape[dim] // blocks)).reshape([-1 if axis == dim else 1 for axis in range(values.ndim)]) for dim in (source, target)]
    chosen = jax.random.permutation(rng, blocks)[partner]
    strong = (owner == chosen) | (owner == (partner + blocks // 2) % blocks)
    return jnp.where(strong, factor * values, values)


def block_scale(own_key, shape, split, smallest, top_value):
    factor_of, own = 1.0, jax.random.fold_in(own_key, 6)
    for position, parts in split:
        heights = jnp.exp(jax.random.uniform(jax.random.fold_in(own, position), (parts,), jnp.float32, smallest / len(split), top_value / len(split)))
        factor_of = factor_of * jnp.repeat(heights, shape[position] // parts).reshape([-1 if axis == position else 1 for axis in range(len(shape))])
    return factor_of


def bell_draw(stream_key, shape, spread, limit, pieces=(), dtype=jnp.bfloat16):
    loudness = block_scale(stream_key, shape, pieces, -0.22, 0.18) if pieces else 1.0
    result = jax.random.normal(stream_key, shape, jnp.float32) * spread * loudness
    return jnp.minimum(jnp.maximum(result, -limit), limit).astype(dtype)


def gaussian_with(stream_key, shape, scale, limit, pieces, heavy, held_as=jnp.bfloat16):
    result = scale * jax.random.normal(stream_key, shape, jnp.float32)
    if pieces:
        result = result * block_scale(stream_key, shape, pieces, -0.22, 0.18)
    return jnp.clip(strengthened(result, jax.random.fold_in(stream_key, 3), *heavy), -limit, limit).astype(held_as)


def setup_inputs(seed: int = 0) -> dict:
    seeds = jax.random.split(jax.random.key(seed), 9)
    return {
        "queries": gaussian_with(seeds[0], (2, BLOCK, HEADS * D), 1.0, 16.0, ((1, 64), (2, 4)), (1, 2, 64, 4.0)),
        "keys": gaussian_with(seeds[1], (BLOCK, HEADS * D), 1.0, 16.0, ((0, 64), (1, 4)), (0, 1, 64, 4.0)),
        "values": bell_draw(seeds[2], (BLOCK, HEADS * D), 1.0, 6.0, ((0, 64), (1, 4))),
        "upstream": bell_draw(seeds[3], (2, BLOCK, HEADS * D), 1.0, 6.0, ((1, 64), (2, 4))),
        "out_gain": jnp.clip(jnp.exp(math.log(2.0) - 1.3862944 * jax.random.uniform(seeds[4], (HEADS * D,), jnp.float32) ** block_scale(seeds[4], (HEADS * D,), ((0, 4),), -0.2, 0.2)), 0.5, 2.0),
        "gate_weight": bell_draw(seeds[5], (HEADS, D, H), D ** -0.5, 0.25, ((0, 4), (1, 64))),
        "up_weight": bell_draw(seeds[6], (HEADS, D, H), D ** -0.5, 0.25, ((0, 4), (1, 64))),
        "down_weight": bell_draw(seeds[7], (HEADS, H, D), H ** -0.5, 0.25, ((0, 4), (1, 64))),
    }


lin_coef = 3.4445
cube_coef = -4.775
fifth_coef = 2.0315
rms_eps = 1e-06
fro_eps = 1e-07

def product(left, right):
    return jnp.dot(left, right, preferred_element_type=jnp.float32)

def across(left, right):
    return lax.dot_general(left, right, (((0,), (0,)), ((), ())), preferred_element_type=jnp.float32)

def against(left, right):
    return lax.dot_general(left, right, (((1,), (1,)), ((), ())), preferred_element_type=jnp.float32)

def fast_forward(keys, values, weights):
    gate_weight, up_weight, down_weight = weights
    gate_pre = product(keys, gate_weight)
    up_pre = product(keys, up_weight)
    sigma = jax.nn.sigmoid(gate_pre)
    active = gate_pre * sigma
    hidden = (active * up_pre).astype(jnp.bfloat16)
    back = -against(values, down_weight)
    slope = sigma * (1.0 + gate_pre * (1.0 - sigma))
    d_gate = (back * up_pre * slope).astype(jnp.bfloat16)
    d_up = (back * active).astype(jnp.bfloat16)
    fast = (across(keys, d_gate), across(keys, d_up), -across(hidden, values))
    saved = (gate_pre, up_pre, sigma, active, hidden, back, slope, d_gate, d_up)
    return (fast, saved)

def fast_second(keys, values, weights, saved, cots):
    gate_weight, up_weight, down_weight = weights
    gate_pre, up_pre, sigma, active, hidden, back, slope, d_gate, d_up = saved
    cot_gate, cot_up, cot_down = cots
    along_gate = product(keys, cot_gate)
    along_up = product(keys, cot_up)
    along_hidden = -against(values, cot_down)
    curve = sigma * (1.0 - sigma) * (2.0 + gate_pre * (1.0 - 2.0 * sigma))
    d_back = (along_gate * up_pre * slope + along_up * active).astype(jnp.bfloat16)
    d_upper = (along_gate * back * slope + along_hidden * active).astype(jnp.bfloat16)
    d_lower = (along_gate * back * up_pre * curve + along_up * back * slope + along_hidden * up_pre * slope).astype(jnp.bfloat16)
    grad_keys = (against(d_gate, cot_gate) + against(d_up, cot_up) + against(d_lower, gate_weight) + against(d_upper, up_weight)).astype(jnp.bfloat16)
    grad_values = (-product(hidden, cot_down) - product(d_back, down_weight)).astype(jnp.bfloat16)
    partial_value = (across(keys, d_lower), across(keys, d_upper), -across(d_back, values))
    return (grad_keys, grad_values, partial_value)

def apply_forward(queries, weights):
    gate_weight, up_weight, down_weight = weights
    gate_pre = product(queries, gate_weight)
    up_pre = product(queries, up_weight)
    sigma = jax.nn.sigmoid(gate_pre)
    hidden = (gate_pre * sigma * up_pre).astype(jnp.bfloat16)
    output = product(hidden, down_weight)
    return (gate_pre, up_pre, sigma, hidden, output)

def apply_backward(queries, weights, saved, upstream, out_gain, inverse_rms, mean_dot):
    gate_weight, up_weight, down_weight = weights
    gate_pre, up_pre, sigma, hidden, output = saved
    weighted = out_gain * upstream.astype(jnp.float32)
    d_output = (inverse_rms[:, None] * weighted - output * (inverse_rms * inverse_rms * inverse_rms * mean_dot)[:, None]).astype(jnp.bfloat16)
    back = against(d_output, down_weight)
    slope = sigma * (1.0 + gate_pre * (1.0 - sigma))
    d_gate = (back * up_pre * slope).astype(jnp.bfloat16)
    d_up = (back * gate_pre * sigma).astype(jnp.bfloat16)
    grad_queries = (against(d_gate, gate_weight) + against(d_up, up_weight)).astype(jnp.bfloat16)
    partial_value = (across(queries, d_gate), across(queries, d_up), across(hidden, d_output))
    return (grad_queries, partial_value)

def schulz_forward(begin):
    current = begin
    saved = []
    for sweep in range(NS_STEPS):
        gram = against(current, current).astype(jnp.bfloat16)
        blend = (cube_coef * gram.astype(jnp.float32) + fifth_coef * product(gram, gram)).astype(jnp.bfloat16)
        following = (lin_coef * current.astype(jnp.float32) + product(blend, current)).astype(jnp.bfloat16)
        saved.append((current, gram, blend))
        current = following
    return (current, saved)

def schulz_backward(cotan, saved):
    current = cotan
    for iterate, gram, blend in reversed(saved):
        cross = against(current, iterate)
        symmetric = (cross + cross.T).astype(jnp.bfloat16)
        bent = product(symmetric, gram)
        mixed = (cube_coef * symmetric.astype(jnp.float32) + fifth_coef * (bent + bent.T)).astype(jnp.bfloat16)
        current = (lin_coef * current.astype(jnp.float32) + product(blend, current) + product(mixed, iterate)).astype(jnp.bfloat16)
    return current

def restore(bottom, fast, root):
    norm = root + fro_eps
    inner = jnp.sum(bottom.astype(jnp.float32) * fast)
    return (bottom.astype(jnp.float32) / norm - fast * (inner / (norm * norm * root))).astype(jnp.bfloat16)

def reference(queries, keys, values, upstream, out_gain, gate_weight, up_weight, down_weight):
    heads = gate_weight.shape[0]
    width = heads * D
    scale = 1.0 / math.sqrt(BLOCK)
    records = []
    power_sums = [jnp.zeros((BLOCK,), jnp.float32), jnp.zeros((BLOCK,), jnp.float32)]
    dot_sums = [jnp.zeros((BLOCK,), jnp.float32), jnp.zeros((BLOCK,), jnp.float32)]
    for head in range(heads):
        lower = head * D
        first = (gate_weight[head], up_weight[head], down_weight[head])
        fast, unused = fast_forward(keys[:, lower:lower + D], values[:, lower:lower + D], first)
        roots = [jnp.sqrt(jnp.sum(item * item)) for item in fast]
        begins = [(fast[which] / (roots[which] + fro_eps)).astype(jnp.bfloat16) for which in range(3)]
        forward = [schulz_forward(begin) for begin in begins]
        second = tuple(((first[which].astype(jnp.float32) - forward[which][0].astype(jnp.float32)).astype(jnp.bfloat16) for which in range(3)))
        for block_index, weights in ((0, first), (1, second)):
            output = apply_forward(queries[block_index][:, lower:lower + D], weights)[4]
            weighted = out_gain[lower:lower + D] * upstream[block_index][:, lower:lower + D].astype(jnp.float32)
            power_sums[block_index] = power_sums[block_index] + lax.optimization_barrier(jnp.sum(output * output, axis=1))
            dot_sums[block_index] = dot_sums[block_index] + lax.optimization_barrier(jnp.sum(weighted * output, axis=1))
        records.append((first, second, fast, roots, forward))
    inverse = [lax.rsqrt(power_sums[which] / width + rms_eps) for which in range(2)]
    means = [dot_sums[which] / width for which in range(2)]
    query_grads, key_grads, value_grads = ([], [], [])
    gate_grads, up_grads, down_grads = ([], [], [])
    for head in range(heads):
        lower = head * D
        first, second, fast, roots, forward = records[head]
        gain_part = out_gain[lower:lower + D]
        block_grads = []
        partials = []
        for block_index, weights in ((0, first), (1, second)):
            local_queries = queries[block_index][:, lower:lower + D]
            saved = apply_forward(local_queries, weights)
            grad_part, partial_value = apply_backward(local_queries, weights, saved, upstream[block_index][:, lower:lower + D], gain_part, inverse[block_index], means[block_index])
            block_grads.append(grad_part)
            partials.append(partial_value)
        tops = [(-partials[1][which]).astype(jnp.bfloat16) for which in range(3)]
        bottoms = [schulz_backward(tops[which], forward[which][1]) for which in range(3)]
        cots = tuple((restore(bottoms[which], fast[which], roots[which]) for which in range(3)))
        local_keys = keys[:, lower:lower + D]
        local_values = values[:, lower:lower + D]
        unused, saved_keys = fast_forward(local_keys, local_values, first)
        grad_key_part, grad_value_part, second_order = fast_second(local_keys, local_values, first, saved_keys, cots)
        totals = [(partials[0][which] + second_order[which] + partials[1][which]) * scale for which in range(3)]
        query_grads.append(jnp.stack(block_grads))
        key_grads.append(grad_key_part)
        value_grads.append(grad_value_part)
        gate_grads.append(totals[0])
        up_grads.append(totals[1])
        down_grads.append(totals[2])
    return (jnp.concatenate(query_grads, axis=2), jnp.concatenate(key_grads, axis=1), jnp.concatenate(value_grads, axis=1), jnp.stack(gate_grads), jnp.stack(up_grads), jnp.stack(down_grads))
```

```python
import math

import jax
import jax.numpy as jnp
from jax import lax
from jax.experimental import pallas as pl
from jax.experimental.pallas import tpu as pltpu
from jax.sharding import PartitionSpec as P

lin_coef = 3.4445
cube_coef = -4.775
fifth_coef = 2.0315
rms_eps = 1e-06
fro_eps = 1e-07

X, Z, HEADS = 4, 8, 4
D = 512
T = 128
HALF = 256
PIECE = 16
ROWS = 128
F32, BF16 = jnp.float32, jnp.bfloat16
MESH = pl.DeviceIdType.MESH


def mm(a, b):
    return jnp.dot(a, b, preferred_element_type=F32)


def mt(a, b):
    return lax.dot_general(a, b, (((1,), (1,)), ((), ())), preferred_element_type=F32)


def sigmoid(v):
    return 1.0 / (1.0 + jnp.exp(-v))


def turned(v):
    return v.astype(F32).T.astype(BF16)


def kernel(
    q_hbm, k_hbm, v_hbm, up_hbm, gain_ref, g_rows, u_rows, d_rows,
    gq_out, gk_out, gv_out, gg_out, gu_out, gd_out,
    q_ref, k_ref, v_ref, up_ref, in_sem,
    wf, wx, w0, gh, pt, w1, a0, b0, x1, a1, b1, cc,
    gk_s, uk_s, back_s, hid_k, hidn_t, rg,
    q1_t, hq1_t, r1, lt, rf,
    oq, gq_s, uq_s, st, sr,
    cs, cr, acc, xs1p, xs1m, xr1l, xr1r, xs2p, xs2m, xr2l, xr2r, xblk, zs, zr,
    piece, norms, fx, fr,
    ag_send, ag_recv, rs_send, rs_recv, st_send, st_recv, pair_send, pair_recv,
):
    tok = lax.axis_index("tok")
    y = lax.axis_index("head")
    c = lax.rem(tok, 2)
    o = 1 - c
    chip = lax.div(tok, 2)
    z = lax.rem(chip, Z)
    x = lax.div(chip, Z)
    xp, xm, x2 = lax.rem(x + 1, X), lax.rem(x + 3, X), lax.rem(x + 2, X)

    def device(x_, z_, c_):
        return ((x_ * Z + z_) * 2 + c_, y)

    partner = device(x, z, o)
    right, left = device(xp, z, c), device(xm, z, c)
    z_to = [device(x, lax.rem(z + step, Z), c) for step in range(1, Z)]
    y_to = [(tok, lax.rem(y + step, HEADS)) for step in range(1, HEADS)]
    mine = pl.ds(pl.multiple_of(c * HALF, HALF), HALF)
    other = pl.ds(pl.multiple_of(o * HALF, HALF), HALF)

    def rows(start, size):
        return pl.ds(pl.multiple_of(start, 16), size)

    loads = [
        pltpu.make_async_copy(source, target, in_sem.at[i])
        for i, (source, target) in enumerate(
            ((k_hbm, k_ref), (v_hbm, v_ref), (q_hbm, q_ref), (up_hbm, up_ref))
        )
    ]
    for load in loads:
        load.start()

    barrier = pltpu.get_barrier_semaphore()
    peers = [partner, right, left] + z_to + y_to
    for peer in peers:
        pl.semaphore_signal(barrier, inc=1, device_id=peer, device_id_type=MESH)
    pl.semaphore_wait(barrier, len(peers))

    sent = []

    def remote(source, target, send, recv, peer):
        return pltpu.make_async_remote_copy(
            src_ref=source, dst_ref=target, send_sem=send, recv_sem=recv,
            device_id=peer, device_id_type=MESH,
        )

    def push(*args):
        copy = remote(*args)
        copy.start()
        sent.append(copy)

    for w, ref in enumerate((g_rows, u_rows, d_rows)):
        wf[w] = ref[0].astype(F32)
    push(
        wf.at[:, :, other], wx.at[:, pl.ds(pl.multiple_of(c * 8, 8), 8), :],
        pair_send.at[0], pair_recv.at[0], partner,
    )
    wx[:, pl.ds(pl.multiple_of(c * 8, 8), 8), :] = wf[:, :, mine]
    remote(
        wf.at[:, :, other], wx.at[:, pl.ds(pl.multiple_of(o * 8, 8), 8), :],
        pair_send.at[0], pair_recv.at[0], partner,
    ).wait_recv()
    w0[:, rows(chip * PIECE, PIECE), mine] = wx[...].astype(BF16)

    def gather(buf, phase):
        def block(w, x_, side, skip=0, size=ROWS):
            return buf.at[w, rows(x_ * ROWS + skip, size), side]

        def go(w, index, ref, peer):
            push(ref, ref, ag_send.at[phase, w, index], ag_recv.at[phase, w, index], peer)

        def come(w, index, ref):
            remote(
                ref, ref, ag_send.at[phase, w, index], ag_recv.at[phase, w, index], partner
            ).wait_recv()

        for w in range(3):
            for step in range(1, Z):
                go(w, step - 1, buf.at[w, rows(chip * PIECE, PIECE), mine], z_to[step - 1])
        yield
        for w in range(3):
            for step in range(1, Z):
                origin = x * ROWS + lax.rem(z + Z - step, Z) * PIECE
                come(w, step - 1, buf.at[w, rows(origin, PIECE), mine])
            go(w, 7, block(w, x, mine), right)
            go(w, 8, block(w, x, mine), left)
            go(w, 11, block(w, x, mine), partner)
        yield
        for w in range(3):
            come(w, 7, block(w, xm, mine))
            go(w, 9, block(w, xm, mine, 0, 64), right)
            come(w, 8, block(w, xp, mine))
            go(w, 10, block(w, xp, mine, 64, 64), left)
            go(w, 12, block(w, xm, mine), partner)
            go(w, 13, block(w, xp, mine), partner)
        yield
        for w in range(3):
            come(w, 9, block(w, x2, mine, 0, 64))
            come(w, 10, block(w, x2, mine, 64, 64))
            go(w, 14, block(w, x2, mine), partner)
        yield
        for w in range(3):
            for index, x_ in ((11, x), (12, xm), (13, xp), (14, x2)):
                come(w, index, block(w, x_, other))
        yield

    def reduce(partial, phase):
        def go(w, index, source, target, peer):
            push(source, target, rs_send.at[phase, w, index], rs_recv.at[phase, w, index], peer)

        def come(w, index, ref):
            remote(
                ref, ref, rs_send.at[phase, w, index], rs_recv.at[phase, w, index], partner
            ).wait_recv()

        for w in range(3):
            cs[phase, w] = partial(w, other).astype(BF16)
            go(w, 0, cs.at[phase, w], cr.at[phase, w], partner)
        for w in range(3):
            acc[w] = partial(w, mine)
        yield
        for w in range(3):
            come(w, 0, cr.at[phase, w])

            def total(x_, skip, w=w):
                span = rows(x_ * ROWS + skip, 64)
                return acc[w, span, :] + cr[phase, w, span, :].astype(F32)

            xs1p[phase, w, :64] = total(x2, 0).astype(BF16)
            xs1p[phase, w, 64:] = total(xp, 64).astype(BF16)
            go(w, 1, xs1p.at[phase, w], xr1l.at[phase, w], right)
            xs1m[phase, w, :64] = total(xm, 0).astype(BF16)
            xs1m[phase, w, 64:] = total(x2, 64).astype(BF16)
            go(w, 2, xs1m.at[phase, w], xr1r.at[phase, w], left)
        yield
        for w in range(3):

            def total(x_, skip, w=w):
                span = rows(x_ * ROWS + skip, 64)
                return acc[w, span, :] + cr[phase, w, span, :].astype(F32)

            come(w, 1, xr1l.at[phase, w])
            xs2p[phase, w] = (total(xp, 0) + xr1l[phase, w, :64].astype(F32)).astype(BF16)
            go(w, 3, xs2p.at[phase, w], xr2l.at[phase, w], right)
            come(w, 2, xr1r.at[phase, w])
            xs2m[phase, w] = (total(xm, 64) + xr1r[phase, w, 64:].astype(F32)).astype(BF16)
            go(w, 4, xs2m.at[phase, w], xr2r.at[phase, w], left)
            xblk[w, :64] = total(x, 0) + xr1r[phase, w, :64].astype(F32)
            xblk[w, 64:] = total(x, 64) + xr1l[phase, w, 64:].astype(F32)
        yield
        for w in range(3):
            come(w, 3, xr2l.at[phase, w])
            come(w, 4, xr2r.at[phase, w])
            xblk[w, :64] = xblk[w, :64] + xr2l[phase, w].astype(F32)
            xblk[w, 64:] = xblk[w, 64:] + xr2r[phase, w].astype(F32)
            zs[phase, w] = xblk[w].astype(BF16)
            for step in range(1, Z):
                target = lax.rem(z + step, Z)
                go(
                    w, 4 + step, zs.at[phase, w, rows(target * PIECE, PIECE), :],
                    zr.at[phase, w, step - 1], z_to[step - 1],
                )
        yield
        for w in range(3):
            total_piece = xblk[w, rows(z * PIECE, PIECE), :]
            for step in range(1, Z):
                come(w, 4 + step, zr.at[phase, w, step - 1])
                total_piece = total_piece + zr[phase, w, step - 1].astype(F32)
            piece[phase, w] = total_piece
        yield

    def run(steps):
        for _ in steps:
            pass

    run(gather(w0, 0))
    for load in loads:
        load.wait()

    keys, values = k_ref[...], v_ref[...]
    gate_pre, up_pre = mm(keys, w0[0]), mm(keys, w0[1])
    back = -mt(values, w0[2])
    gk_s[...], uk_s[...], back_s[...] = gate_pre, up_pre, back
    sigma = sigmoid(gate_pre)
    active = gate_pre * sigma
    hidden = (active * up_pre).astype(BF16)
    slope = sigma * (1.0 + gate_pre * (1.0 - sigma))
    rg[0] = (back * up_pre * slope).astype(BF16)
    rg[1] = (back * active).astype(BF16)
    rg[2] = values
    hid_k[...] = hidden
    hidn_t[...] = turned(-hidden.astype(F32))
    lt[0, :, T:] = turned(keys)
    rf[2, T:] = values

    def fast_partial(w, side):
        left_t = hidn_t[...] if w == 2 else lt[0, :, T:]
        return mm(left_t, rg[w, :, side])

    def apply_forward(b, weights):
        queries = q_ref[b]
        pre, upper = mm(queries, weights[0]), mm(queries, weights[1])
        sq = sigmoid(pre)
        hidden_q = (pre * sq * upper).astype(BF16)
        output = mm(hidden_q, weights[2])
        gq_s[...], uq_s[...], oq[...] = pre, upper, output
        weighted = gain_ref[...] * up_ref[b].astype(F32)
        power = jnp.sum(output * output, axis=1, keepdims=True)
        dots = jnp.sum(weighted * output, axis=1, keepdims=True)
        lane = lax.broadcasted_iota(jnp.int32, (T, T), 1)
        both = jnp.where(lane == 0, jnp.broadcast_to(power, (T, T)), jnp.broadcast_to(dots, (T, T)))
        st[b] = both.T[:8]
        for step in range(1, HEADS):
            push(
                st.at[b], sr.at[b, step - 1], st_send.at[b, step - 1], st_recv.at[b, step - 1],
                y_to[step - 1],
            )
        return hidden_q

    def apply_backward(b, weights, right_refs):
        total = st[b]
        for step in range(1, HEADS):
            remote(
                st.at[b], sr.at[b, step - 1], st_send.at[b, step - 1], st_recv.at[b, step - 1],
                y_to[step - 1],
            ).wait_recv()
            total = total + sr[b, step - 1]
        mean = total * (1.0 / (HEADS * D))
        inverse = lax.rsqrt(mean[0:1] + rms_eps)
        ratio = inverse * inverse * inverse * mean[1:2]
        down = jnp.where(
            lax.broadcasted_iota(jnp.int32, (T, T), 0) == 0,
            jnp.broadcast_to(inverse, (T, T)),
            jnp.broadcast_to(ratio, (T, T)),
        ).T
        weighted = gain_ref[...] * up_ref[b].astype(F32)
        d_output = (down[:, 0:1] * weighted - oq[...] * down[:, 1:2]).astype(BF16)
        back_q = mt(d_output, weights[2])
        pre, upper = gq_s[...], uq_s[...]
        sq = sigmoid(pre)
        right_refs[0][...] = (back_q * upper * (sq * (1.0 + pre * (1.0 - sq)))).astype(BF16)
        right_refs[1][...] = (back_q * pre * sq).astype(BF16)
        right_refs[2][...] = d_output

    def query_grad(b, weights, right_refs):
        gq_out[b] = (
            mt(right_refs[0][...], weights[0]) + mt(right_refs[1][...], weights[1])
        ).astype(BF16)

    steps = reduce(fast_partial, 0)
    next(steps)
    hidden_q = apply_forward(0, w0)
    lt[0, :, :T] = turned(q_ref[0])
    lt[1, :, :T] = turned(hidden_q)
    next(steps)
    first_refs = [rf.at[w, pl.ds(0, T), :] for w in range(3)]
    apply_backward(0, w0, first_refs)
    next(steps)
    query_grad(0, w0, first_refs)
    q1_t[...] = turned(q_ref[1])
    next(steps)
    next(steps)
    gh[:, rows(chip * PIECE, PIECE), mine] = piece[0].astype(BF16)
    run(gather(gh, 1))

    def schulz(w, carry):
        fast = gh[w]
        fast32 = fast.astype(F32)
        power = jnp.sum(jnp.sum(fast32 * fast32, axis=1, keepdims=True), axis=0, keepdims=True)
        root = jnp.sqrt(power)
        norm = root + fro_eps
        inv = 1.0 / norm
        norms[w, 0:8] = jnp.broadcast_to(root, (8, 128))
        norms[w, 8:16] = jnp.broadcast_to(norm, (8, 128))
        gram = (mt(fast, fast) * (inv * inv)).astype(BF16)
        a0[w] = gram
        blend = (cube_coef * gram.astype(F32) + fifth_coef * mm(gram, gram)).astype(BF16)
        b0[w] = blend
        iterate = (inv * (lin_coef * gh[w].astype(F32) + mm(blend, gh[w]))).astype(BF16)
        x1[w] = iterate
        gram = mt(iterate, iterate).astype(BF16)
        a1[w] = gram
        blend = (cube_coef * gram.astype(F32) + fifth_coef * mm(gram, gram)).astype(BF16)
        b1[w] = blend
        final = (lin_coef * x1[w].astype(F32) + mm(blend, x1[w])).astype(BF16)
        w1[w] = (w0[w].astype(F32) - final.astype(F32)).astype(BF16)
        return carry

    lax.fori_loop(0, 3, schulz, 0)

    hidden_q = apply_forward(1, w1)
    hq1_t[...] = turned(hidden_q)
    second_refs = [r1.at[w] for w in range(3)]
    apply_backward(1, w1, second_refs)

    def second_partial(w, side):
        left_t = hq1_t[...] if w == 2 else q1_t[...]
        return mm(left_t, r1[w, :, side])

    steps = reduce(second_partial, 1)
    next(steps)
    query_grad(1, w1, second_refs)
    run(steps)
    pt[:, rows(chip * PIECE, PIECE), mine] = (-piece[1]).astype(BF16)
    run(gather(pt, 2))

    def schulz_back(w, carry):
        root, norm = norms[w, 0:1, 0:1], norms[w, 8:9, 0:1]
        inv = 1.0 / norm

        def sweep(current, iterate, gram, blend, scale):
            cross = mt(current, iterate) + mt(iterate, current)
            if scale is not None:
                cross = cross * scale
            symmetric = cross.astype(BF16)
            bent = mm(symmetric, gram) + mm(gram, symmetric)
            mixed = (cube_coef * symmetric.astype(F32) + fifth_coef * bent).astype(BF16)
            follow = mm(mixed, iterate)
            if scale is not None:
                follow = follow * scale
            return (lin_coef * current.astype(F32) + mm(blend, current) + follow).astype(BF16)

        current = sweep(pt[w], x1[w], a1[w], b1[w], None)
        bottom = sweep(current, gh[w], a0[w], b0[w], inv).astype(F32)
        fast = gh[w].astype(F32)
        inner = jnp.sum(jnp.sum(bottom * fast, axis=1, keepdims=True), axis=0, keepdims=True)
        cc[w] = (bottom * inv - fast * (inner / (norm * norm * root))).astype(BF16)
        return carry

    lax.fori_loop(0, 3, schulz_back, 0)

    keys, values = k_ref[...], v_ref[...]
    along_gate, along_up = mm(keys, cc[0]), mm(keys, cc[1])
    along_hidden = -mt(values, cc[2])
    gate_pre, up_pre, back = gk_s[...], uk_s[...], back_s[...]
    sigma = sigmoid(gate_pre)
    active = gate_pre * sigma
    slope = sigma * (1.0 + gate_pre * (1.0 - sigma))
    curve = sigma * (1.0 - sigma) * (2.0 + gate_pre * (1.0 - 2.0 * sigma))
    d_back = (along_gate * up_pre * slope + along_up * active).astype(BF16)
    rf[1, T:] = (along_gate * back * slope + along_hidden * active).astype(BF16)
    rf[0, T:] = (
        along_gate * back * up_pre * curve + along_up * back * slope + along_hidden * up_pre * slope
    ).astype(BF16)
    lt[1, :, T:] = turned(-d_back.astype(F32))
    r1[2] = d_back

    def last_partial(w, side):
        return mm(lt[w // 2], rf[w, :, side])

    steps = reduce(last_partial, 2)
    next(steps)
    gk_out[...] = (
        mt(rg[0], cc[0]) + mt(rg[1], cc[1]) + mt(rf[0, T:], w0[0]) + mt(rf[1, T:], w0[1])
    ).astype(BF16)
    next(steps)
    gv_out[...] = (-mm(hid_k[...], cc[2]) - mm(r1[2], w0[2])).astype(BF16)
    run(steps)

    scale = 1.0 / math.sqrt(8192)
    fx[...] = (piece[1] + piece[2]) * scale
    push(
        fx.at[:, pl.ds(pl.multiple_of(o * 8, 8), 8), :], fr.at[:, :, mine],
        pair_send.at[1], pair_recv.at[1], partner,
    )
    fr[:, :, mine] = fx[:, pl.ds(pl.multiple_of(c * 8, 8), 8), :]
    remote(
        fx.at[:, pl.ds(pl.multiple_of(o * 8, 8), 8), :], fr.at[:, :, other],
        pair_send.at[1], pair_recv.at[1], partner,
    ).wait_recv()
    for w, out in enumerate((gg_out, gu_out, gd_out)):
        out[0] = fr[w]
    for copy in sent:
        copy.wait_send()


def per_device(queries, keys, values, upstream, out_gain, gate_weight, up_weight, down_weight):
    vmem = pl.BlockSpec(memory_space=pltpu.VMEM)
    hbm = pl.BlockSpec(memory_space=pl.ANY)
    square = pltpu.VMEM((3, D, D), BF16)
    wide = pltpu.VMEM((T, D), F32)
    dma = pltpu.SemaphoreType.DMA
    scratch = [
        pltpu.VMEM((2, T, D), BF16), pltpu.VMEM((T, D), BF16), pltpu.VMEM((T, D), BF16),
        pltpu.VMEM((2, T, D), BF16), dma((4,)),
        pltpu.VMEM((3, 8, D), F32), pltpu.VMEM((3, PIECE, HALF), F32),
    ] + [square] * 10 + [
        wide, wide, wide, pltpu.VMEM((T, D), BF16), pltpu.VMEM((D, T), BF16),
        pltpu.VMEM((3, T, D), BF16),
        pltpu.VMEM((D, T), BF16), pltpu.VMEM((D, T), BF16), pltpu.VMEM((3, T, D), BF16),
        pltpu.VMEM((2, D, 2 * T), BF16), pltpu.VMEM((3, 2 * T, D), BF16),
        wide, wide, wide, pltpu.VMEM((2, 8, 128), F32), pltpu.VMEM((2, 3, 8, 128), F32),
        pltpu.VMEM((3, 3, D, HALF), BF16), pltpu.VMEM((3, 3, D, HALF), BF16),
        pltpu.VMEM((3, D, HALF), F32),
    ] + [pltpu.VMEM((3, 3, 128, HALF), BF16)] * 4 + [pltpu.VMEM((3, 3, 64, HALF), BF16)] * 4 + [
        pltpu.VMEM((3, 128, HALF), F32), pltpu.VMEM((3, 3, 128, HALF), BF16),
        pltpu.VMEM((3, 3, Z - 1, PIECE, HALF), BF16),
        pltpu.VMEM((3, 3, PIECE, HALF), F32), pltpu.VMEM((3, 16, 128), F32),
        pltpu.VMEM((3, PIECE, HALF), F32), pltpu.VMEM((3, 8, D), F32),
        dma((3, 3, 15)), dma((3, 3, 15)), dma((3, 3, 12)), dma((3, 3, 12)),
        dma((2, 3)), dma((2, 3)), dma((2,)), dma((2,)),
    ]
    grad = jax.ShapeDtypeStruct((1, 8, D), F32)
    return pl.pallas_call(
        kernel,
        out_shape=(
            jax.ShapeDtypeStruct((2, T, D), BF16), jax.ShapeDtypeStruct((T, D), BF16),
            jax.ShapeDtypeStruct((T, D), BF16), grad, grad, grad,
        ),
        in_specs=[hbm] * 4 + [vmem] * 4,
        out_specs=[vmem] * 6,
        scratch_shapes=scratch,
        compiler_params=pltpu.CompilerParams(
            collective_id=0, has_side_effects=True, vmem_limit_bytes=60 * 1024 * 1024
        ),
    )(queries, keys, values, upstream, out_gain[None], gate_weight, up_weight, down_weight)


def solution(mesh):
    in_specs = (
        P(None, "tok", "head"),
        P("tok", "head"),
        P("tok", "head"),
        P(None, "tok", "head"),
        P("head"),
        P("head", "tok", None),
        P("head", "tok", None),
        P("head", "tok", None),
    )
    out_specs = (
        P(None, "tok", "head"),
        P("tok", "head"),
        P("tok", "head"),
        P("head", "tok", None),
        P("head", "tok", None),
        P("head", "tok", None),
    )
    return jax.shard_map(
        per_device, mesh=mesh, in_specs=in_specs, out_specs=out_specs, check_vma=False
    )
```

```python
import math

import jax
import jax.numpy as jnp
from jax import lax
from jax.experimental import pallas as pl
from jax.experimental.pallas import tpu as pltpu
from jax.sharding import PartitionSpec as P

lin_coef = 3.4445
cube_coef = -4.775
fifth_coef = 2.0315
rms_eps = 1e-06
fro_eps = 1e-07

X, Z, HEADS = 4, 8, 4
D = 512
T = 128
HALF = 256
PIECE = 16
ROWS = 128
F32, BF16 = jnp.float32, jnp.bfloat16
MESH = pl.DeviceIdType.MESH


def mm(a, b):
    return jnp.dot(a, b, preferred_element_type=F32)


def mt(a, b):
    return lax.dot_general(a, b, (((1,), (1,)), ((), ())), preferred_element_type=F32)


def sigmoid(v):
    return 1.0 / (1.0 + jnp.exp(-v))


def turned(v):
    return v.astype(F32).T.astype(BF16)


def kernel(
    q_hbm, k_hbm, v_hbm, up_hbm, gain_ref, g_rows, u_rows, d_rows,
    gq_out, gk_out, gv_out, gg_out, gu_out, gd_out,
    q_ref, k_ref, v_ref, up_ref, in_sem,
    wf, wx, w0, gh, pt, w1, a0, b0, x1, a1, b1, cc,
    gk_s, uk_s, back_s, hid_k, hidn_t, rg,
    q1_t, hq1_t, r1, lt, rf,
    oq, gq_s, uq_s, st, sr,
    cs, cr, acc, s1, q1, s2, q2, sx, qx, sz, qz, xblk,
    piece, norms, fx, fr,
    ag_send, ag_recv, rs_send, rs_recv, ar_send, ar_recv, st_send, st_recv, pair_send, pair_recv,
):
    tok = lax.axis_index("tok")
    y = lax.axis_index("head")
    c = lax.rem(tok, 2)
    o = 1 - c
    chip = lax.div(tok, 2)
    z = lax.rem(chip, Z)
    x = lax.div(chip, Z)

    def device(x_, z_, c_):
        return ((x_ * Z + z_) * 2 + c_, y)

    partner = device(x, z, o)

    def x_by(step):
        return device(lax.rem(x + step, X), z, c)

    def z_by(step):
        return device(x, lax.rem(z + step + Z, Z), c)

    y_to = [(tok, lax.rem(y + step, HEADS)) for step in range(1, HEADS)]
    mine = pl.ds(pl.multiple_of(c * HALF, HALF), HALF)
    other = pl.ds(pl.multiple_of(o * HALF, HALF), HALF)

    def rows(start, size):
        return pl.ds(pl.multiple_of(start, 16), size)

    loads = [
        pltpu.make_async_copy(source, target, in_sem.at[i])
        for i, (source, target) in enumerate(
            ((k_hbm, k_ref), (v_hbm, v_ref), (q_hbm, q_ref), (up_hbm, up_ref))
        )
    ]
    for load in loads:
        load.start()

    barrier = pltpu.get_barrier_semaphore()
    peers = [partner] + [x_by(step) for step in range(1, X)] + [z_by(step) for step in range(1, Z)] + y_to
    for peer in peers:
        pl.semaphore_signal(barrier, inc=1, device_id=peer, device_id_type=MESH)
    pl.semaphore_wait(barrier, len(peers))

    sent = []

    def remote(source, target, send, recv, peer):
        return pltpu.make_async_remote_copy(
            src_ref=source, dst_ref=target, send_sem=send, recv_sem=recv,
            device_id=peer, device_id_type=MESH,
        )

    def push(*args):
        copy = remote(*args)
        copy.start()
        sent.append(copy)

    for w, ref in enumerate((g_rows, u_rows, d_rows)):
        wf[w] = ref[0].astype(F32)
    push(
        wf.at[:, :, other], wx.at[:, pl.ds(pl.multiple_of(c * 8, 8), 8), :],
        pair_send.at[0], pair_recv.at[0], partner,
    )
    wx[:, pl.ds(pl.multiple_of(c * 8, 8), 8), :] = wf[:, :, mine]
    remote(
        wf.at[:, :, other], wx.at[:, pl.ds(pl.multiple_of(o * 8, 8), 8), :],
        pair_send.at[0], pair_recv.at[0], partner,
    ).wait_recv()
    w0[:, rows(chip * PIECE, PIECE), mine] = wx[...].astype(BF16)

    def part(buf, x_, z_, side):
        return buf.at[:, rows((x_ * Z + lax.rem(z_ + Z, Z)) * PIECE, PIECE), side]

    def gather(buf):
        def go(index, ref, peer):
            push(ref, ref, ag_send.at[index], ag_recv.at[index], peer)

        def come(index, ref):
            remote(ref, ref, ag_send.at[index], ag_recv.at[index], partner).wait_recv()

        def block(x_, side):
            return buf.at[:, rows(x_ * ROWS, ROWS), side]

        offsets = (0, -1, 1, -2, 2, -3, 3, 4)

        def across(g):
            ref = part(buf, x, z + offsets[g], mine)
            for step in (1, 3, 2):
                go(6 + 3 * g + step, ref, x_by(step))

        own = part(buf, x, z, mine)
        for g in range(1, Z):
            go(g - 1, own, z_by(-offsets[g]))
        across(0)
        yield
        for g in range(1, Z):
            come(g - 1, part(buf, x, z + offsets[g], mine))
            across(g)
        go(31, block(x, mine), partner)
        yield
        for step in (1, 3, 2):
            x_ = lax.rem(x + X - step, X)
            for g in range(Z):
                come(6 + 3 * g + step, part(buf, x_, z + offsets[g], mine))
            go(31 + step, block(x_, mine), partner)
        for step in (0, 1, 3, 2):
            come(31 + step, block(lax.rem(x + X - step, X), other))
        yield

    def reduce(partial):
        def go(index, source, target, peer):
            push(source, target, rs_send.at[index], rs_recv.at[index], peer)

        def come(index, ref):
            remote(ref, ref, rs_send.at[index], rs_recv.at[index], partner).wait_recv()

        offsets = (4, 3, -3, 2, -2, 1, -1, 0)

        def total(x_, j):
            span = rows((x_ * Z + lax.rem(z + offsets[j] + Z, Z)) * PIECE, PIECE)
            return acc[:, span, :] + cr[2, :, span, :].astype(F32)

        def first(j):
            for step in (2, 1, 3):
                s1[j, step - 1] = total(lax.rem(x + step, X), j).astype(BF16)
                go(2 + 3 * j + step, s1.at[j, step - 1], q1.at[j, step - 1], x_by(step))

        def second(j):
            result = total(x, j)
            for step in (1, 3, 2):
                come(2 + 3 * j + step, q1.at[j, step - 1])
                result = result + q1[j, step - 1].astype(F32)
            if j < Z - 1:
                s2[j] = result.astype(BF16)
                go(27 + j, s2.at[j], q2.at[j], z_by(offsets[j]))
            else:
                fx[...] = result

        for w in range(3):
            cs[2, w] = partial(w, other).astype(BF16)
            go(w, cs.at[2, w], cr.at[2, w], partner)
        for w in range(3):
            acc[w] = partial(w, mine)
        yield
        for w in range(3):
            come(w, cr.at[2, w])
        for j in range(Z):
            first(j)
        yield
        for j in range(Z):
            second(j)
        result = fx[...]
        for j in range(Z - 1):
            come(27 + j, q2.at[j])
            result = result + q2[j].astype(F32)
        fx[...] = result
        yield

    def combine(partial, phase, buf, sign):
        def go(w, index, source, target, peer):
            push(source, target, ar_send.at[phase, w, index], ar_recv.at[phase, w, index], peer)

        def come(w, index, ref):
            remote(ref, ref, ar_send.at[phase, w, index], ar_recv.at[phase, w, index], partner).wait_recv()

        def block(w, x_, side):
            return buf.at[w, rows(x_ * ROWS, ROWS), side]

        def own(w, z_):
            return buf.at[w, rows((x * Z + z_) * PIECE, PIECE), mine]

        for w in range(3):
            cs[phase, w] = partial(w, other).astype(BF16)
            go(w, 0, cs.at[phase, w], cr.at[phase, w], partner)
        for w in range(3):
            acc[w] = partial(w, mine)
        yield
        for w in range(3):
            come(w, 0, cr.at[phase, w])
            for step in (2, 1, 3):
                span = rows(lax.rem(x + step, X) * ROWS, ROWS)
                sx[phase, w, step - 1] = (
                    acc[w, span, :] + cr[phase, w, span, :].astype(F32)
                ).astype(BF16)
                go(w, step, sx.at[phase, w, step - 1], qx.at[phase, w, step - 1], x_by(step))
        yield
        for w in range(3):
            span = rows(x * ROWS, ROWS)
            result = acc[w, span, :] + cr[phase, w, span, :].astype(F32)
            for step in (1, 3, 2):
                come(w, step, qx.at[phase, w, step - 1])
                result = result + qx[phase, w, step - 1].astype(F32)
            xblk[w] = result
            sz[phase, w] = result.astype(BF16)
            for step in (4, 3, 5, 2, 6, 1, 7):
                target = lax.rem(z + step, Z)
                go(
                    w, 3 + step, sz.at[phase, w, rows(target * PIECE, PIECE), :],
                    qz.at[phase, w, step - 1], z_by(step),
                )
        yield
        for w in range(3):
            result = xblk[w, rows(z * PIECE, PIECE), :]
            for step in (1, 7, 2, 6, 3, 5, 4):
                come(w, 3 + step, qz.at[phase, w, step - 1])
                result = result + qz[phase, w, step - 1].astype(F32)
            piece[phase, w] = result
            buf[w, rows(chip * PIECE, PIECE), mine] = (sign * result).astype(BF16)
            for step in (4, 3, 5, 2, 6, 1, 7):
                go(w, 10 + step, own(w, z), own(w, z), z_by(step))
        yield
        for w in range(3):
            for step in (1, 7, 2, 6, 3, 5, 4):
                come(w, 10 + step, own(w, lax.rem(z + Z - step, Z)))
            for step in (2, 1, 3):
                go(w, 17 + step, block(w, x, mine), block(w, x, mine), x_by(step))
            go(w, 21, block(w, x, mine), block(w, x, mine), partner)
        yield

    def finish(w, phase, buf):
        for step in (1, 3, 2):
            ref = buf.at[w, rows(lax.rem(x + X - step, X) * ROWS, ROWS), mine]
            remote(
                ref, ref, ar_send.at[phase, w, 17 + step], ar_recv.at[phase, w, 17 + step], partner
            ).wait_recv()
            remote(
                ref, ref, ar_send.at[phase, w, 21 + step], ar_recv.at[phase, w, 21 + step], partner
            ).start()

    def follow(w, phase, buf):
        for step in (0, 1, 3, 2):
            ref = buf.at[w, rows(lax.rem(x + X - step, X) * ROWS, ROWS), other]
            remote(
                ref, ref, ar_send.at[phase, w, 21 + step], ar_recv.at[phase, w, 21 + step], partner
            ).wait_recv()

    def leave(w, phase, buf):
        for step in (1, 3, 2):
            ref = buf.at[w, rows(lax.rem(x + X - step, X) * ROWS, ROWS), mine]
            remote(
                ref, ref, ar_send.at[phase, w, 21 + step], ar_recv.at[phase, w, 21 + step], partner
            ).wait_send()

    def run(steps):
        for _ in steps:
            pass

    run(gather(w0))
    for load in loads:
        load.wait()

    keys, values = k_ref[...], v_ref[...]
    gate_pre, up_pre = mm(keys, w0[0]), mm(keys, w0[1])
    back = -mt(values, w0[2])
    gk_s[...], uk_s[...], back_s[...] = gate_pre, up_pre, back
    sigma = sigmoid(gate_pre)
    active = gate_pre * sigma
    hidden = (active * up_pre).astype(BF16)
    slope = sigma * (1.0 + gate_pre * (1.0 - sigma))
    rg[0] = (back * up_pre * slope).astype(BF16)
    rg[1] = (back * active).astype(BF16)
    rg[2] = values
    hid_k[...] = hidden
    hidn_t[...] = turned(-hidden.astype(F32))
    lt[0, :, T:] = turned(keys)
    rf[2, T:] = values

    def fast_partial(w, side):
        left_t = hidn_t[...] if w == 2 else lt[0, :, T:]
        return mm(left_t, rg[w, :, side])

    def apply_forward(b, weights):
        queries = q_ref[b]
        pre, upper = mm(queries, weights[0]), mm(queries, weights[1])
        sq = sigmoid(pre)
        hidden_q = (pre * sq * upper).astype(BF16)
        output = mm(hidden_q, weights[2])
        gq_s[...], uq_s[...], oq[...] = pre, upper, output
        weighted = gain_ref[...] * up_ref[b].astype(F32)
        power = jnp.sum(output * output, axis=1, keepdims=True)
        dots = jnp.sum(weighted * output, axis=1, keepdims=True)
        lane = lax.broadcasted_iota(jnp.int32, (T, T), 1)
        both = jnp.where(lane == 0, jnp.broadcast_to(power, (T, T)), jnp.broadcast_to(dots, (T, T)))
        st[b] = both.T[:8]
        for step in range(1, HEADS):
            push(
                st.at[b], sr.at[b, step - 1], st_send.at[b, step - 1], st_recv.at[b, step - 1],
                y_to[step - 1],
            )
        return hidden_q

    def apply_backward(b, weights, right_refs):
        total = st[b]
        for step in range(1, HEADS):
            remote(
                st.at[b], sr.at[b, step - 1], st_send.at[b, step - 1], st_recv.at[b, step - 1],
                y_to[step - 1],
            ).wait_recv()
            total = total + sr[b, step - 1]
        mean = total * (1.0 / (HEADS * D))
        inverse = lax.rsqrt(mean[0:1] + rms_eps)
        ratio = inverse * inverse * inverse * mean[1:2]
        down = jnp.where(
            lax.broadcasted_iota(jnp.int32, (T, T), 0) == 0,
            jnp.broadcast_to(inverse, (T, T)),
            jnp.broadcast_to(ratio, (T, T)),
        ).T
        weighted = gain_ref[...] * up_ref[b].astype(F32)
        d_output = (down[:, 0:1] * weighted - oq[...] * down[:, 1:2]).astype(BF16)
        back_q = mt(d_output, weights[2])
        pre, upper = gq_s[...], uq_s[...]
        sq = sigmoid(pre)
        right_refs[0][...] = (back_q * upper * (sq * (1.0 + pre * (1.0 - sq)))).astype(BF16)
        right_refs[1][...] = (back_q * pre * sq).astype(BF16)
        right_refs[2][...] = d_output

    def query_grad(b, weights, right_refs):
        gq_out[b] = (
            mt(right_refs[0][...], weights[0]) + mt(right_refs[1][...], weights[1])
        ).astype(BF16)

    first_refs = [rf.at[w, pl.ds(0, T), :] for w in range(3)]
    steps = combine(fast_partial, 0, gh, 1.0)
    next(steps)
    next(steps)
    hidden_q = apply_forward(0, w0)
    next(steps)
    lt[0, :, :T] = turned(q_ref[0])
    lt[1, :, :T] = turned(hidden_q)
    next(steps)
    apply_backward(0, w0, first_refs)
    next(steps)
    q1_t[...] = turned(q_ref[1])
    finish(0, 0, gh)

    def schulz(w, carry):
        follow(w, 0, gh)
        fast = gh[w]
        fast32 = fast.astype(F32)
        power = jnp.sum(jnp.sum(fast32 * fast32, axis=1, keepdims=True), axis=0, keepdims=True)
        root = jnp.sqrt(power)
        norm = root + fro_eps
        inv = 1.0 / norm
        norms[w, 0:8] = jnp.broadcast_to(root, (8, 128))
        norms[w, 8:16] = jnp.broadcast_to(norm, (8, 128))
        gram = (mt(fast, fast) * (inv * inv)).astype(BF16)
        a0[w] = gram
        blend = (cube_coef * gram.astype(F32) + fifth_coef * mm(gram, gram)).astype(BF16)
        b0[w] = blend
        iterate = (inv * (lin_coef * gh[w].astype(F32) + mm(blend, gh[w]))).astype(BF16)
        x1[w] = iterate

        @pl.when(w < 2)
        def _():
            finish(w + 1, 0, gh)

        gram = mt(x1[w], x1[w]).astype(BF16)
        a1[w] = gram
        blend = (cube_coef * gram.astype(F32) + fifth_coef * mm(gram, gram)).astype(BF16)
        b1[w] = blend
        final = (lin_coef * x1[w].astype(F32) + mm(blend, x1[w])).astype(BF16)
        w1[w] = (w0[w].astype(F32) - final.astype(F32)).astype(BF16)
        return carry

    lax.fori_loop(0, 3, schulz, 0)

    hidden_q = apply_forward(1, w1)
    hq1_t[...] = turned(hidden_q)
    second_refs = [r1.at[w] for w in range(3)]
    apply_backward(1, w1, second_refs)

    def second_partial(w, side):
        left_t = hq1_t[...] if w == 2 else q1_t[...]
        return mm(left_t, r1[w, :, side])

    steps = combine(second_partial, 1, pt, -1.0)
    next(steps)
    next(steps)
    query_grad(1, w1, second_refs)
    next(steps)
    query_grad(0, w0, first_refs)
    for _ in steps:
        pass
    finish(0, 1, pt)

    def schulz_back(w, carry):
        follow(w, 1, pt)
        root, norm = norms[w, 0:1, 0:1], norms[w, 8:9, 0:1]
        inv = 1.0 / norm

        def sweep(current, iterate, gram, blend, scale):
            cross = mt(current, iterate)
            cross = cross + cross.T
            if scale is not None:
                cross = cross * scale
            symmetric = cross.astype(BF16)
            bent = mm(symmetric, gram)
            bent = bent + bent.T
            mixed = (cube_coef * symmetric.astype(F32) + fifth_coef * bent).astype(BF16)
            follow = mm(mixed, iterate)
            if scale is not None:
                follow = follow * scale
            return (lin_coef * current.astype(F32) + mm(blend, current) + follow).astype(BF16)

        cc[w] = sweep(pt[w], x1[w], a1[w], b1[w], None)

        @pl.when(w < 2)
        def _():
            finish(w + 1, 1, pt)

        bottom = sweep(cc[w], gh[w], a0[w], b0[w], inv).astype(F32)
        fast = gh[w].astype(F32)
        inner = jnp.sum(jnp.sum(bottom * fast, axis=1, keepdims=True), axis=0, keepdims=True)
        cc[w] = (bottom * inv - fast * (inner / (norm * norm * root))).astype(BF16)
        return carry

    lax.fori_loop(0, 3, schulz_back, 0)

    keys, values = k_ref[...], v_ref[...]
    along_gate, along_up = mm(keys, cc[0]), mm(keys, cc[1])
    along_hidden = -mt(values, cc[2])
    gate_pre, up_pre, back = gk_s[...], uk_s[...], back_s[...]
    sigma = sigmoid(gate_pre)
    active = gate_pre * sigma
    slope = sigma * (1.0 + gate_pre * (1.0 - sigma))
    curve = sigma * (1.0 - sigma) * (2.0 + gate_pre * (1.0 - 2.0 * sigma))
    d_back = (along_gate * up_pre * slope + along_up * active).astype(BF16)
    rf[1, T:] = (along_gate * back * slope + along_hidden * active).astype(BF16)
    rf[0, T:] = (
        along_gate * back * up_pre * curve + along_up * back * slope + along_hidden * up_pre * slope
    ).astype(BF16)
    lt[1, :, T:] = turned(-d_back.astype(F32))
    r1[2] = d_back

    def last_partial(w, side):
        return mm(lt[w // 2], rf[w, :, side])

    steps = reduce(last_partial)
    next(steps)
    gk_out[...] = (
        mt(rg[0], cc[0]) + mt(rg[1], cc[1]) + mt(rf[0, T:], w0[0]) + mt(rf[1, T:], w0[1])
    ).astype(BF16)
    next(steps)
    gv_out[...] = (-mm(hid_k[...], cc[2]) - mm(r1[2], w0[2])).astype(BF16)
    run(steps)

    scale = 1.0 / math.sqrt(8192)
    fx[...] = (piece[1] + fx[...]) * scale
    push(
        fx.at[:, pl.ds(pl.multiple_of(o * 8, 8), 8), :], fr.at[:, :, mine],
        pair_send.at[1], pair_recv.at[1], partner,
    )
    fr[:, :, mine] = fx[:, pl.ds(pl.multiple_of(c * 8, 8), 8), :]
    remote(
        fx.at[:, pl.ds(pl.multiple_of(o * 8, 8), 8), :], fr.at[:, :, other],
        pair_send.at[1], pair_recv.at[1], partner,
    ).wait_recv()
    for w, out in enumerate((gg_out, gu_out, gd_out)):
        out[0] = fr[w]
    for copy in sent:
        copy.wait_send()
    for phase, buf in enumerate((gh, pt)):
        for w in range(3):
            leave(w, phase, buf)


def hand_on(*refs):
    for source, target in zip(refs[:6], refs[6:]):
        target[...] = source[...]


def per_device(queries, keys, values, upstream, out_gain, gate_weight, up_weight, down_weight):
    vmem = pl.BlockSpec(memory_space=pltpu.VMEM)
    hbm = pl.BlockSpec(memory_space=pl.ANY)
    square = pltpu.VMEM((3, D, D), BF16)
    wide = pltpu.VMEM((T, D), F32)
    dma = pltpu.SemaphoreType.DMA
    scratch = [
        pltpu.VMEM((2, T, D), BF16), pltpu.VMEM((T, D), BF16), pltpu.VMEM((T, D), BF16),
        pltpu.VMEM((2, T, D), BF16), dma((4,)),
        pltpu.VMEM((3, 8, D), F32), pltpu.VMEM((3, PIECE, HALF), F32),
    ] + [square] * 10 + [
        wide, wide, wide, pltpu.VMEM((T, D), BF16), pltpu.VMEM((D, T), BF16),
        pltpu.VMEM((3, T, D), BF16),
        pltpu.VMEM((D, T), BF16), pltpu.VMEM((D, T), BF16), pltpu.VMEM((3, T, D), BF16),
        pltpu.VMEM((2, D, 2 * T), BF16), pltpu.VMEM((3, 2 * T, D), BF16),
        wide, wide, wide, pltpu.VMEM((2, 8, 128), F32), pltpu.VMEM((2, 3, 8, 128), F32),
        pltpu.VMEM((3, 3, D, HALF), BF16), pltpu.VMEM((3, 3, D, HALF), BF16),
        pltpu.VMEM((3, D, HALF), F32),
    ] + [pltpu.VMEM((Z, 3, 3, PIECE, HALF), BF16)] * 2 + [pltpu.VMEM((Z - 1, 3, PIECE, HALF), BF16)] * 2 + [
        pltpu.VMEM((2, 3, 3, ROWS, HALF), BF16), pltpu.VMEM((2, 3, 3, ROWS, HALF), BF16),
        pltpu.VMEM((2, 3, ROWS, HALF), BF16), pltpu.VMEM((2, 3, Z - 1, PIECE, HALF), BF16),
        pltpu.VMEM((3, ROWS, HALF), F32),
        pltpu.VMEM((2, 3, PIECE, HALF), F32), pltpu.VMEM((3, 16, 128), F32),
        pltpu.VMEM((3, PIECE, HALF), F32), pltpu.VMEM((3, 8, D), F32),
        dma((35,)), dma((35,)), dma((34,)), dma((34,)), dma((2, 3, 25)), dma((2, 3, 25)),
        dma((2, 3)), dma((2, 3)), dma((2,)), dma((2,)),
    ]
    grad = jax.ShapeDtypeStruct((1, 8, D), F32)
    shapes = (
        jax.ShapeDtypeStruct((2, T, D), BF16), jax.ShapeDtypeStruct((T, D), BF16),
        jax.ShapeDtypeStruct((T, D), BF16), grad, grad, grad,
    )
    outs = pl.pallas_call(
        kernel,
        out_shape=shapes,
        in_specs=[hbm] * 4 + [vmem] * 4,
        out_specs=[vmem] * 6,
        scratch_shapes=scratch,
        compiler_params=pltpu.CompilerParams(
            collective_id=0, has_side_effects=True, vmem_limit_bytes=60 * 1024 * 1024
        ),
    )(queries, keys, values, upstream, out_gain[None], gate_weight, up_weight, down_weight)
    return pl.pallas_call(
        hand_on, out_shape=shapes, in_specs=[vmem] * 6, out_specs=[vmem] * 6,
    )(*outs)


def solution(mesh):
    in_specs = (
        P(None, "tok", "head"),
        P("tok", "head"),
        P("tok", "head"),
        P(None, "tok", "head"),
        P("head"),
        P("head", "tok", None),
        P("head", "tok", None),
        P("head", "tok", None),
    )
    out_specs = (
        P(None, "tok", "head"),
        P("tok", "head"),
        P("tok", "head"),
        P("head", "tok", None),
        P("head", "tok", None),
        P("head", "tok", None),
    )
    return jax.shard_map(
        per_device, mesh=mesh, in_specs=in_specs, out_specs=out_specs, check_vma=False
    )
```

```python
import math

import jax
import jax.numpy as jnp
from jax import lax
from jax.experimental import pallas as pl
from jax.experimental.pallas import tpu as pltpu
from jax.sharding import PartitionSpec as P

lin_coef = 3.4445
cube_coef = -4.775
fifth_coef = 2.0315
rms_eps = 1e-06
fro_eps = 1e-07

X, Z, HEADS = 4, 8, 4
D = 512
BLOCK = 8192
T = 128
HALF = 256
PIECE = 16
ROWS = 128
F32, BF16 = jnp.float32, jnp.bfloat16
MESH = pl.DeviceIdType.MESH


def mm(a, b):
    return jnp.dot(a, b, preferred_element_type=F32)


def mt(a, b):
    return lax.dot_general(a, b, (((1,), (1,)), ((), ())), preferred_element_type=F32)


def sigmoid(v):
    return 1.0 / (1.0 + jnp.exp(-v))


def turned(v):
    return v.astype(F32).T.astype(BF16)


def kernel(
    q_hbm, k_hbm, v_hbm, up_hbm, gain_hbm, g_rows, u_rows, d_rows,
    gq_out, gk_out, gv_out, gg_out, gu_out, gd_out,
    q_ref, k_ref, v_ref, up_ref, gain_ref, wr, in_sem,
    wf, wx, w0, w1, a0, a1, cc, be0, be1, yx0, yx1,
    gk_s, uk_s, back_s, hid_k, hidn_t, rg,
    q1_t, hq1_t, r1, lt, rf,
    oq, gq_s, uq_s, st, sr,
    cs, cr, acc, s1, q1, s2, q2, s2f, sx, qx, sz, qz, xblk,
    piece, norms, fx, fr,
    ag_send, ag_recv, rs_send, rs_recv, ar_send, ar_recv, st_send, st_recv, pair_send, pair_recv,
):
    low, high = pl.ds(0, D), pl.ds(D, D)
    gh, pt, x1 = yx0.at[:, high, :], yx1.at[:, low, :], yx1.at[:, high, :]
    b0, b1 = be0.at[:, :, low], be1.at[:, :, low]
    tok = lax.axis_index("tok")
    y = lax.axis_index("head")
    c = lax.rem(tok, 2)
    o = 1 - c
    chip = lax.div(tok, 2)
    z = lax.rem(chip, Z)
    x = lax.div(chip, Z)

    def device(x_, z_, c_):
        return ((x_ * Z + z_) * 2 + c_, y)

    partner = device(x, z, o)

    def x_by(step):
        return device(lax.rem(x + step, X), z, c)

    def z_by(step, core=c):
        return device(x, lax.rem(z + step + Z, Z), core)

    y_to = [(tok, lax.rem(y + step, HEADS)) for step in range(1, HEADS)]
    mine = pl.ds(pl.multiple_of(c * HALF, HALF), HALF)
    other = pl.ds(pl.multiple_of(o * HALF, HALF), HALF)

    def rows(start, size):
        return pl.ds(pl.multiple_of(start, 16), size)

    loads = [
        pltpu.make_async_copy(source, target, in_sem.at[i])
        for i, (source, target) in enumerate(
            (
                (g_rows.at[0], wr.at[0]), (u_rows.at[0], wr.at[1]), (d_rows.at[0], wr.at[2]),
                (k_hbm, k_ref), (v_hbm, v_ref), (q_hbm, q_ref), (up_hbm, up_ref),
                (gain_hbm, gain_ref),
            )
        )
    ]
    for load in loads:
        load.start()

    barrier = pltpu.get_barrier_semaphore()
    peers = [partner] + [x_by(step) for step in range(1, X)] + y_to
    for step in range(1, Z):
        peers += [z_by(step), z_by(step, o)]
    for peer in peers:
        pl.semaphore_signal(barrier, inc=1, device_id=peer, device_id_type=MESH)
    for w in range(3):
        loads[w].wait()
        wf[w] = wr[w].astype(F32)
    pl.semaphore_wait(barrier, len(peers))

    sent = []

    def remote(source, target, send, recv, peer):
        return pltpu.make_async_remote_copy(
            src_ref=source, dst_ref=target, send_sem=send, recv_sem=recv,
            device_id=peer, device_id_type=MESH,
        )

    def push(*args):
        copy = remote(*args)
        copy.start()
        sent.append(copy)

    push(
        wf.at[:, :, other], wx.at[:, pl.ds(pl.multiple_of(c * 8, 8), 8), :],
        pair_send.at[0], pair_recv.at[0], partner,
    )
    wx[:, pl.ds(pl.multiple_of(c * 8, 8), 8), :] = wf[:, :, mine]
    remote(
        wf.at[:, :, other], wx.at[:, pl.ds(pl.multiple_of(o * 8, 8), 8), :],
        pair_send.at[0], pair_recv.at[0], partner,
    ).wait_recv()
    w0[:, rows(chip * PIECE, PIECE), mine] = wx[...].astype(BF16)

    def part(buf, x_, z_, side):
        return buf.at[:, rows((x_ * Z + lax.rem(z_ + Z, Z)) * PIECE, PIECE), side]

    def gather(buf):
        def go(index, ref, peer):
            push(ref, ref, ag_send.at[index], ag_recv.at[index], peer)

        def come(index, ref):
            remote(ref, ref, ag_send.at[index], ag_recv.at[index], partner).wait_recv()

        def block(x_, side):
            return buf.at[:, rows(x_ * ROWS, ROWS), side]

        offsets = (0, -1, 1, -2, 2, -3, 3, 4)

        def across(g):
            ref = part(buf, x, z + offsets[g], mine)
            for step in (1, 3, 2):
                go(6 + 3 * g + step, ref, x_by(step))

        own = part(buf, x, z, mine)
        for g in range(1, Z):
            go(g - 1, own, z_by(-offsets[g]))
        across(0)
        yield
        for g in range(1, Z):
            come(g - 1, part(buf, x, z + offsets[g], mine))
            across(g)
        go(31, block(x, mine), partner)
        yield
        for step in (1, 3, 2):
            x_ = lax.rem(x + X - step, X)
            for g in range(Z):
                come(6 + 3 * g + step, part(buf, x_, z + offsets[g], mine))
            go(31 + step, block(x_, mine), partner)
        for step in (0, 1, 3, 2):
            come(31 + step, block(lax.rem(x + X - step, X), other))
        yield

    def reduce(partial):
        def go(index, source, target, peer):
            push(source, target, rs_send.at[index], rs_recv.at[index], peer)

        def come(index, ref):
            remote(ref, ref, rs_send.at[index], rs_recv.at[index], partner).wait_recv()

        offsets = (4, 3, -3, 2, -2, 1, -1, 0)

        def total(x_, j):
            span = rows((x_ * Z + lax.rem(z + offsets[j] + Z, Z)) * PIECE, PIECE)
            return acc[:, span, :] + cr[2, :, span, :].astype(F32)

        def first(j):
            for step in (2, 1, 3):
                s1[j, step - 1] = total(lax.rem(x + step, X), j).astype(BF16)
                go(2 + 3 * j + step, s1.at[j, step - 1], q1.at[j, step - 1], x_by(step))

        def second(j):
            result = total(x, j)
            for step in (1, 3, 2):
                come(2 + 3 * j + step, q1.at[j, step - 1])
                result = result + q1[j, step - 1].astype(F32)
            if j < Z - 1:
                s2f[...] = result
                for index, core in enumerate((c, o)):
                    rows8 = s2f[:, pl.ds(pl.multiple_of(core * 8, 8), 8), :]
                    s2[j, index] = jnp.concatenate(
                        [rows8[:, :, :128], rows8[:, :, 128:]], axis=1
                    ).astype(BF16)
                    go(27 + 2 * j + index, s2.at[j, index], q2.at[j, index], z_by(offsets[j], core))
            else:
                fx[...] = result + piece[1]
                push(
                    fx.at[:, pl.ds(pl.multiple_of(o * 8, 8), 8), :], fr.at[:, :, mine],
                    pair_send.at[1], pair_recv.at[1], partner,
                )

        for w in range(3):
            cs[2, w] = partial(w, other).astype(BF16)
            go(w, cs.at[2, w], cr.at[2, w], partner)
        for w in range(3):
            acc[w] = partial(w, mine)
        yield
        for w in range(3):
            come(w, cr.at[2, w])
        for j in range(Z):
            first(j)
        yield
        for j in range(Z):
            second(j)
        sides = [fx[:, pl.ds(pl.multiple_of(c * 8, 8), 8), :], None]
        for j in range(Z - 1):
            for index in range(2):
                come(27 + 2 * j + index, q2.at[j, index])
        remote(
            fx.at[:, pl.ds(pl.multiple_of(o * 8, 8), 8), :], fr.at[:, :, other],
            pair_send.at[1], pair_recv.at[1], partner,
        ).wait_recv()
        sides[1] = fr[:, :, other]
        for j in range(Z - 1):
            for index in range(2):
                packed = q2[j, index].astype(F32)
                sides[index] = sides[index] + jnp.concatenate([packed[:, :8], packed[:, 8:]], axis=2)
        scale = 1.0 / math.sqrt(BLOCK)
        fr[:, :, mine] = sides[0] * scale
        fr[:, :, other] = sides[1] * scale
        yield

    def combine(partial, phase, buf, sign):
        def go(w, index, source, target, peer):
            push(source, target, ar_send.at[phase, w, index], ar_recv.at[phase, w, index], peer)

        def come(w, index, ref):
            remote(ref, ref, ar_send.at[phase, w, index], ar_recv.at[phase, w, index], partner).wait_recv()

        def block(w, x_, side):
            return buf.at[w, rows(x_ * ROWS, ROWS), side]

        def own(w, z_):
            return buf.at[w, rows((x * Z + z_) * PIECE, PIECE), mine]

        for w in range(3):
            cs[phase, w] = partial(w, other).astype(BF16)
            go(w, 0, cs.at[phase, w], cr.at[phase, w], partner)
        for w in range(3):
            acc[w] = partial(w, mine)
        yield
        for w in range(3):
            come(w, 0, cr.at[phase, w])
            for step in (2, 1, 3):
                span = rows(lax.rem(x + step, X) * ROWS, ROWS)
                sx[phase, w, step - 1] = (
                    acc[w, span, :] + cr[phase, w, span, :].astype(F32)
                ).astype(BF16)
                go(w, step, sx.at[phase, w, step - 1], qx.at[phase, w, step - 1], x_by(step))
        yield
        for w in range(3):
            span = rows(x * ROWS, ROWS)
            result = acc[w, span, :] + cr[phase, w, span, :].astype(F32)
            for step in (1, 3, 2):
                come(w, step, qx.at[phase, w, step - 1])
                result = result + qx[phase, w, step - 1].astype(F32)
            xblk[w] = result
            sz[phase, w] = result.astype(BF16)
            for step in (4, 3, 5, 2, 6, 1, 7):
                target = lax.rem(z + step, Z)
                go(
                    w, 3 + step, sz.at[phase, w, rows(target * PIECE, PIECE), :],
                    qz.at[phase, w, step - 1], z_by(step),
                )
        yield
        for w in range(3):
            result = xblk[w, rows(z * PIECE, PIECE), :]
            for step in (1, 7, 2, 6, 3, 5, 4):
                come(w, 3 + step, qz.at[phase, w, step - 1])
                result = result + qz[phase, w, step - 1].astype(F32)
            piece[phase, w] = result
            buf[w, rows(chip * PIECE, PIECE), mine] = (sign * result).astype(BF16)
            for step in (4, 3, 5, 2, 6, 1, 7):
                go(w, 10 + step, own(w, z), own(w, z), z_by(step))
        yield
        for w in range(3):
            for step in (1, 7, 2, 6, 3, 5, 4):
                come(w, 10 + step, own(w, lax.rem(z + Z - step, Z)))
            for step in (2, 1, 3):
                go(w, 17 + step, block(w, x, mine), block(w, x, mine), x_by(step))
            go(w, 21, block(w, x, mine), block(w, x, mine), partner)
        yield

    def finish(w, phase, buf):
        for step in (1, 3, 2):
            ref = buf.at[w, rows(lax.rem(x + X - step, X) * ROWS, ROWS), mine]
            remote(
                ref, ref, ar_send.at[phase, w, 17 + step], ar_recv.at[phase, w, 17 + step], partner
            ).wait_recv()
            remote(
                ref, ref, ar_send.at[phase, w, 21 + step], ar_recv.at[phase, w, 21 + step], partner
            ).start()

    def follow(w, phase, buf):
        for step in (0, 1, 3, 2):
            ref = buf.at[w, rows(lax.rem(x + X - step, X) * ROWS, ROWS), other]
            remote(
                ref, ref, ar_send.at[phase, w, 21 + step], ar_recv.at[phase, w, 21 + step], partner
            ).wait_recv()

    def leave(w, phase, buf):
        for step in (1, 3, 2):
            ref = buf.at[w, rows(lax.rem(x + X - step, X) * ROWS, ROWS), mine]
            remote(
                ref, ref, ar_send.at[phase, w, 21 + step], ar_recv.at[phase, w, 21 + step], partner
            ).wait_send()

    def run(steps):
        for _ in steps:
            pass

    run(gather(w0))
    for load in loads[3:]:
        load.wait()

    keys, values = k_ref[...], v_ref[...]
    gate_pre, up_pre = mm(keys, w0[0]), mm(keys, w0[1])
    back = -mt(values, w0[2])
    gk_s[...], uk_s[...], back_s[...] = gate_pre, up_pre, back
    sigma = sigmoid(gate_pre)
    active = gate_pre * sigma
    hidden = (active * up_pre).astype(BF16)
    slope = sigma * (1.0 + gate_pre * (1.0 - sigma))
    rg[0] = (back * up_pre * slope).astype(BF16)
    rg[1] = (back * active).astype(BF16)
    rg[2] = values
    hid_k[...] = hidden
    hidn_t[...] = turned(-hidden.astype(F32))
    lt[0, :, T:] = turned(keys)
    rf[2, T:] = values

    def fast_partial(w, side):
        left_t = hidn_t[...] if w == 2 else lt[0, :, T:]
        return mm(left_t, rg[w, :, side])

    def apply_forward(b, weights):
        queries = q_ref[b]
        pre, upper = mm(queries, weights[0]), mm(queries, weights[1])
        sq = sigmoid(pre)
        hidden_q = (pre * sq * upper).astype(BF16)
        output = mm(hidden_q, weights[2])
        gq_s[...], uq_s[...], oq[...] = pre, upper, output
        weighted = gain_ref[...] * up_ref[b].astype(F32)
        power = jnp.sum(output * output, axis=1, keepdims=True)
        dots = jnp.sum(weighted * output, axis=1, keepdims=True)
        lane = lax.broadcasted_iota(jnp.int32, (T, T), 1)
        both = jnp.where(lane == 0, jnp.broadcast_to(power, (T, T)), jnp.broadcast_to(dots, (T, T)))
        st[b] = both.T[:8]
        for step in range(1, HEADS):
            push(
                st.at[b], sr.at[b, step - 1], st_send.at[b, step - 1], st_recv.at[b, step - 1],
                y_to[step - 1],
            )
        return hidden_q

    def apply_backward(b, weights, right_refs):
        total = st[b]
        for step in range(1, HEADS):
            remote(
                st.at[b], sr.at[b, step - 1], st_send.at[b, step - 1], st_recv.at[b, step - 1],
                y_to[step - 1],
            ).wait_recv()
            total = total + sr[b, step - 1]
        mean = total * (1.0 / (HEADS * D))
        inverse = lax.rsqrt(mean[0:1] + rms_eps)
        ratio = inverse * inverse * inverse * mean[1:2]
        down = jnp.where(
            lax.broadcasted_iota(jnp.int32, (T, T), 0) == 0,
            jnp.broadcast_to(inverse, (T, T)),
            jnp.broadcast_to(ratio, (T, T)),
        ).T
        weighted = gain_ref[...] * up_ref[b].astype(F32)
        d_output = (down[:, 0:1] * weighted - oq[...] * down[:, 1:2]).astype(BF16)
        back_q = mt(d_output, weights[2])
        pre, upper = gq_s[...], uq_s[...]
        sq = sigmoid(pre)
        right_refs[0][...] = (back_q * upper * (sq * (1.0 + pre * (1.0 - sq)))).astype(BF16)
        right_refs[1][...] = (back_q * pre * sq).astype(BF16)
        right_refs[2][...] = d_output

    def query_grad(b, weights, right_refs):
        gq_out[b] = (
            mt(right_refs[0][...], weights[0]) + mt(right_refs[1][...], weights[1])
        ).astype(BF16)

    first_refs = [rf.at[w, pl.ds(0, T), :] for w in range(3)]
    steps = combine(fast_partial, 0, gh, 1.0)
    next(steps)
    next(steps)
    hidden_q = apply_forward(0, w0)
    next(steps)
    lt[0, :, :T] = turned(q_ref[0])
    lt[1, :, :T] = turned(hidden_q)
    next(steps)
    apply_backward(0, w0, first_refs)
    next(steps)
    q1_t[...] = turned(q_ref[1])
    finish(0, 0, gh)

    def schulz(w, carry):
        follow(w, 0, gh)
        fast = gh[w]
        fast32 = fast.astype(F32)
        power = jnp.sum(jnp.sum(fast32 * fast32, axis=1, keepdims=True), axis=0, keepdims=True)
        root = jnp.sqrt(power)
        norm = root + fro_eps
        inv = 1.0 / norm
        norms[w, 0:8] = jnp.broadcast_to(root, (8, 128))
        norms[w, 8:16] = jnp.broadcast_to(norm, (8, 128))
        gram = (mt(fast, fast) * (inv * inv)).astype(BF16)
        a0[w] = gram
        blend = (cube_coef * gram.astype(F32) + fifth_coef * mm(gram, gram)).astype(BF16)
        b0[w] = blend
        iterate = (inv * (lin_coef * gh[w].astype(F32) + mm(blend, gh[w]))).astype(BF16)
        x1[w] = iterate

        @pl.when(w < 2)
        def _():
            finish(w + 1, 0, gh)

        gram = mt(x1[w], x1[w]).astype(BF16)
        a1[w] = gram
        blend = (cube_coef * gram.astype(F32) + fifth_coef * mm(gram, gram)).astype(BF16)
        b1[w] = blend
        final = (lin_coef * x1[w].astype(F32) + mm(blend, x1[w])).astype(BF16)
        w1[w] = (w0[w].astype(F32) - final.astype(F32)).astype(BF16)
        return carry

    lax.fori_loop(0, 3, schulz, 0)

    hidden_q = apply_forward(1, w1)
    hq1_t[...] = turned(hidden_q)
    second_refs = [r1.at[w] for w in range(3)]
    apply_backward(1, w1, second_refs)

    def second_partial(w, side):
        left_t = hq1_t[...] if w == 2 else q1_t[...]
        return mm(left_t, r1[w, :, side])

    steps = combine(second_partial, 1, pt, -1.0)
    next(steps)
    next(steps)
    query_grad(1, w1, second_refs)
    next(steps)
    query_grad(0, w0, first_refs)
    for _ in steps:
        pass
    finish(0, 1, pt)

    def schulz_back(w, carry):
        follow(w, 1, pt)
        root, norm = norms[w, 0:1, 0:1], norms[w, 8:9, 0:1]
        inv = 1.0 / norm

        def sweep(pair, gram, both, scale):
            cross = mt(pair[w, low], pair[w, high])
            cross = cross + cross.T
            if scale is not None:
                cross = cross * scale
            symmetric = cross.astype(BF16)
            bent = mm(symmetric, gram)
            bent = bent + bent.T
            mixed = cube_coef * symmetric.astype(F32) + fifth_coef * bent
            if scale is not None:
                mixed = mixed * scale
            both[w, :, high] = mixed.astype(BF16)
            return (lin_coef * pair[w, low].astype(F32) + mm(both[w], pair[w])).astype(BF16)

        yx0[w, low] = sweep(yx1, a1[w], be1, None)

        @pl.when(w < 2)
        def _():
            finish(w + 1, 1, pt)

        bottom = sweep(yx0, a0[w], be0, inv).astype(F32)
        fast = gh[w].astype(F32)
        inner = jnp.sum(jnp.sum(bottom * fast, axis=1, keepdims=True), axis=0, keepdims=True)
        cc[w] = (bottom * inv - fast * (inner / (norm * norm * root))).astype(BF16)
        return carry

    lax.fori_loop(0, 3, schulz_back, 0)

    keys, values = k_ref[...], v_ref[...]
    along_gate, along_up = mm(keys, cc[0]), mm(keys, cc[1])
    along_hidden = -mt(values, cc[2])
    gate_pre, up_pre, back = gk_s[...], uk_s[...], back_s[...]
    sigma = sigmoid(gate_pre)
    active = gate_pre * sigma
    slope = sigma * (1.0 + gate_pre * (1.0 - sigma))
    curve = sigma * (1.0 - sigma) * (2.0 + gate_pre * (1.0 - 2.0 * sigma))
    d_back = (along_gate * up_pre * slope + along_up * active).astype(BF16)
    rf[1, T:] = (along_gate * back * slope + along_hidden * active).astype(BF16)
    rf[0, T:] = (
        along_gate * back * up_pre * curve + along_up * back * slope + along_hidden * up_pre * slope
    ).astype(BF16)
    lt[1, :, T:] = turned(-d_back.astype(F32))
    r1[2] = d_back

    def last_partial(w, side):
        return mm(lt[w // 2], rf[w, :, side])

    steps = reduce(last_partial)
    next(steps)
    gk_out[...] = (
        mt(rg[0], cc[0]) + mt(rg[1], cc[1]) + mt(rf[0, T:], w0[0]) + mt(rf[1, T:], w0[1])
    ).astype(BF16)
    next(steps)
    gv_out[...] = (-mm(hid_k[...], cc[2]) - mm(r1[2], w0[2])).astype(BF16)
    run(steps)

    for w, out in enumerate((gg_out, gu_out, gd_out)):
        out[0] = fr[w]
    for copy in sent:
        copy.wait_send()
    for phase, buf in enumerate((gh, pt)):
        for w in range(3):
            leave(w, phase, buf)


def hand_on(*refs):
    copies = [
        pltpu.make_async_copy(refs[i], refs[6 + i], refs[12].at[i]) for i in range(6)
    ]
    for copy in copies:
        copy.start()
    for copy in copies:
        copy.wait()


def per_device(queries, keys, values, upstream, out_gain, gate_weight, up_weight, down_weight):
    vmem = pl.BlockSpec(memory_space=pltpu.VMEM)
    hbm = pl.BlockSpec(memory_space=pl.ANY)
    square = pltpu.VMEM((3, D, D), BF16)
    wide = pltpu.VMEM((T, D), F32)
    dma = pltpu.SemaphoreType.DMA
    scratch = [
        pltpu.VMEM((2, T, D), BF16), pltpu.VMEM((T, D), BF16), pltpu.VMEM((T, D), BF16),
        pltpu.VMEM((2, T, D), BF16), pltpu.VMEM((1, D), F32), pltpu.VMEM((3, 8, D), BF16), dma((8,)),
        pltpu.VMEM((3, 8, D), F32), pltpu.VMEM((3, PIECE, HALF), F32),
    ] + [square] * 5 + [pltpu.VMEM((3, D, 2 * D), BF16)] * 2 + [pltpu.VMEM((3, 2 * D, D), BF16)] * 2 + [
        wide, wide, wide, pltpu.VMEM((T, D), BF16), pltpu.VMEM((D, T), BF16),
        pltpu.VMEM((3, T, D), BF16),
        pltpu.VMEM((D, T), BF16), pltpu.VMEM((D, T), BF16), pltpu.VMEM((3, T, D), BF16),
        pltpu.VMEM((2, D, 2 * T), BF16), pltpu.VMEM((3, 2 * T, D), BF16),
        wide, wide, wide, pltpu.VMEM((2, 8, 128), F32), pltpu.VMEM((2, 3, 8, 128), F32),
        pltpu.VMEM((3, 3, D, HALF), BF16), pltpu.VMEM((3, 3, D, HALF), BF16),
        pltpu.VMEM((3, D, HALF), F32),
    ] + [pltpu.VMEM((Z, 3, 3, PIECE, HALF), BF16)] * 2 + [pltpu.VMEM((Z - 1, 2, 3, PIECE, 128), BF16)] * 2 + [
        pltpu.VMEM((3, PIECE, HALF), F32),
        pltpu.VMEM((2, 3, 3, ROWS, HALF), BF16), pltpu.VMEM((2, 3, 3, ROWS, HALF), BF16),
        pltpu.VMEM((2, 3, ROWS, HALF), BF16), pltpu.VMEM((2, 3, Z - 1, PIECE, HALF), BF16),
        pltpu.VMEM((3, ROWS, HALF), F32),
        pltpu.VMEM((2, 3, PIECE, HALF), F32), pltpu.VMEM((3, 16, 128), F32),
        pltpu.VMEM((3, PIECE, HALF), F32), pltpu.VMEM((3, 8, D), F32),
        dma((35,)), dma((35,)), dma((41,)), dma((41,)), dma((2, 3, 25)), dma((2, 3, 25)),
        dma((2, 3)), dma((2, 3)), dma((2,)), dma((2,)),
    ]
    grad = jax.ShapeDtypeStruct((1, 8, D), F32)
    shapes = (
        jax.ShapeDtypeStruct((2, T, D), BF16), jax.ShapeDtypeStruct((T, D), BF16),
        jax.ShapeDtypeStruct((T, D), BF16), grad, grad, grad,
    )
    outs = pl.pallas_call(
        kernel,
        out_shape=tuple(pltpu.VMEM(shape.shape, shape.dtype) for shape in shapes),
        in_specs=[hbm] * 8,
        out_specs=[vmem] * 6,
        scratch_shapes=scratch,
        compiler_params=pltpu.CompilerParams(
            collective_id=0, has_side_effects=True, vmem_limit_bytes=60 * 1024 * 1024
        ),
    )(queries, keys, values, upstream, out_gain[None], gate_weight, up_weight, down_weight)
    return pl.pallas_call(
        hand_on, out_shape=shapes, in_specs=[vmem] * 6, out_specs=[hbm] * 6,
        scratch_shapes=[dma((6,))],
    )(*[pltpu.with_memory_space_constraint(out, pltpu.VMEM) for out in outs])


def solution(mesh):
    in_specs = (
        P(None, "tok", "head"),
        P("tok", "head"),
        P("tok", "head"),
        P(None, "tok", "head"),
        P("head"),
        P("head", "tok", None),
        P("head", "tok", None),
        P("head", "tok", None),
    )
    out_specs = (
        P(None, "tok", "head"),
        P("tok", "head"),
        P("tok", "head"),
        P("head", "tok", None),
        P("head", "tok", None),
        P("head", "tok", None),
    )
    return jax.shard_map(
        per_device, mesh=mesh, in_specs=in_specs, out_specs=out_specs, check_vma=False
    )
```

```python
import math

import jax
import jax.numpy as jnp
from jax import lax
from jax.experimental import pallas as pl
from jax.experimental.pallas import tpu as pltpu
from jax.sharding import PartitionSpec as P

lin_coef = 3.4445
cube_coef = -4.775
fifth_coef = 2.0315
rms_eps = 1e-06
fro_eps = 1e-07

X, Z, HEADS = 4, 8, 4
D = 512
BLOCK = 8192
T = 128
HALF = 256
PIECE = 16
ROWS = 128
F32, BF16 = jnp.float32, jnp.bfloat16
MESH = pl.DeviceIdType.MESH


def mm(a, b):
    return jnp.dot(a, b, preferred_element_type=F32)


def mt(a, b):
    return lax.dot_general(a, b, (((1,), (1,)), ((), ())), preferred_element_type=F32)


def sigmoid(v):
    return 1.0 / (1.0 + jnp.exp(-v))


def turned(v):
    return v.astype(F32).T.astype(BF16)


def kernel(
    q_hbm, k_hbm, v_hbm, up_hbm, gain_hbm, g_rows, u_rows, d_rows,
    gq_out, gk_out, gv_out, gg_out, gu_out, gd_out,
    q_ref, k_ref, v_ref, up_ref, gain_ref, wr, in_sem,
    wq, w0, w1, a0, a1, cc, be0, be1, yx0, yx1,
    gk_s, uk_s, back_s, hid_k, hidn_t, rg,
    q1_t, hq1_t, r1, lt, rf,
    oq, gq_s, uq_s, st, sr,
    cs, cr, acc, s1, q1, s2, q2, s2f, sx, qx, sz, qz, xblk,
    piece, norms, fx, fr,
    ag_send, ag_recv, rs_send, rs_recv, ar_send, ar_recv, st_send, st_recv, pair_send, pair_recv,
):
    low, high = pl.ds(0, D), pl.ds(D, D)
    gh, pt, x1 = yx0.at[:, high, :], yx1.at[:, low, :], yx1.at[:, high, :]
    b0, b1 = be0.at[:, :, low], be1.at[:, :, low]
    tok = lax.axis_index("tok")
    y = lax.axis_index("head")
    c = lax.rem(tok, 2)
    o = 1 - c
    chip = lax.div(tok, 2)
    z = lax.rem(chip, Z)
    x = lax.div(chip, Z)

    def device(x_, z_, c_):
        return ((x_ * Z + z_) * 2 + c_, y)

    partner = device(x, z, o)

    def x_by(step):
        return device(lax.rem(x + step, X), z, c)

    def z_by(step, core=c):
        return device(x, lax.rem(z + step + Z, Z), core)

    y_to = [(tok, lax.rem(y + step, HEADS)) for step in range(1, HEADS)]
    mine = pl.ds(pl.multiple_of(c * HALF, HALF), HALF)
    other = pl.ds(pl.multiple_of(o * HALF, HALF), HALF)

    def rows(start, size):
        return pl.ds(pl.multiple_of(start, 16), size)

    loads = [
        pltpu.make_async_copy(source, target, in_sem.at[i])
        for i, (source, target) in enumerate(
            (
                (g_rows.at[0], wr.at[0]), (u_rows.at[0], wr.at[1]), (d_rows.at[0], wr.at[2]),
                (k_hbm, k_ref), (v_hbm, v_ref), (q_hbm, q_ref), (up_hbm, up_ref),
                (gain_hbm, gain_ref),
            )
        )
    ]
    barrier = pltpu.get_barrier_semaphore()
    peers = [partner] + [x_by(step) for step in range(1, X)] + y_to
    for step in range(1, Z):
        peers += [z_by(step), z_by(step, o)]
    for peer in peers:
        pl.semaphore_signal(barrier, inc=1, device_id=peer, device_id_type=MESH)
    for load in loads:
        load.start()
    for w in range(3):
        loads[w].wait()
    pl.semaphore_wait(barrier, len(peers))

    sent = []

    def remote(source, target, send, recv, peer):
        return pltpu.make_async_remote_copy(
            src_ref=source, dst_ref=target, send_sem=send, recv_sem=recv,
            device_id=peer, device_id_type=MESH,
        )

    def drain(count):
        for copy in sent[:count]:
            copy.wait_send()
        del sent[:count]

    def push(*args):
        copy = remote(*args)
        copy.start()
        sent.append(copy)

    def gather():
        def go(index, source, target, peer):
            push(source, target, ag_send.at[index], ag_recv.at[index], peer)

        def come(index, ref):
            remote(ref, ref, ag_send.at[index], ag_recv.at[index], partner).wait_recv()

        def part(x_, z_):
            return wq.at[:, x_ * Z + lax.rem(z_ + Z, Z), c]

        def block(x_, core):
            return wq.at[:, pl.ds(x_ * Z, Z), core]

        offsets = (0, -1, 1, -2, 2, -3, 3, 4)

        def across(g):
            ref = part(x, z + offsets[g])
            for step in (1, 3, 2):
                go(6 + 3 * g + step, wr if g == 0 else ref, ref, x_by(step))

        for g in range(1, Z):
            go(g - 1, wr, part(x, z), z_by(-offsets[g]))
        across(0)
        wq[:, chip, c] = wr[...]
        for g in range(1, Z):
            come(g - 1, part(x, z + offsets[g]))
            across(g)
        go(31, block(x, c), block(x, c), partner)
        for step in (1, 3, 2):
            x_ = lax.rem(x + X - step, X)
            for g in range(Z):
                come(6 + 3 * g + step, part(x_, z + offsets[g]))
            go(31 + step, block(x_, c), block(x_, c), partner)
        for step in (0, 1, 3, 2):
            x_ = lax.rem(x + X - step, X)
            come(31 + step, block(x_, o))
            for w in range(3):
                whole = wq[w, pl.ds(x_ * Z, Z)].astype(F32)
                w0[w, rows(x_ * ROWS, ROWS), :] = whole.reshape(ROWS, D).astype(BF16)

    def reduce(partial):
        def go(index, source, target, peer):
            push(source, target, rs_send.at[index], rs_recv.at[index], peer)

        def come(index, ref):
            remote(ref, ref, rs_send.at[index], rs_recv.at[index], partner).wait_recv()

        offsets = (4, 3, -3, 2, -2, 1, -1, 0)

        def total(x_, j):
            span = rows((x_ * Z + lax.rem(z + offsets[j] + Z, Z)) * PIECE, PIECE)
            return acc[:, span, :] + cr[2, :, span, :].astype(F32)

        def first(j):
            for step in (2, 1, 3):
                s1[j, step - 1] = total(lax.rem(x + step, X), j).astype(BF16)
                go(2 + 3 * j + step, s1.at[j, step - 1], q1.at[j, step - 1], x_by(step))

        def second(j):
            result = total(x, j)
            for step in (1, 3, 2):
                come(2 + 3 * j + step, q1.at[j, step - 1])
                result = result + q1[j, step - 1].astype(F32)
            if j < Z - 1:
                s2f[...] = result
                for index, core in enumerate((c, o)):
                    rows8 = s2f[:, pl.ds(pl.multiple_of(core * 8, 8), 8), :]
                    s2[j, index] = jnp.concatenate(
                        [rows8[:, :, :128], rows8[:, :, 128:]], axis=1
                    ).astype(BF16)
                    go(27 + 2 * j + index, s2.at[j, index], q2.at[j, index], z_by(offsets[j], core))
            else:
                fx[...] = result + piece[1]
                push(
                    fx.at[:, pl.ds(pl.multiple_of(o * 8, 8), 8), :], fr.at[:, :, mine],
                    pair_send.at[1], pair_recv.at[1], partner,
                )

        for w in range(3):
            cs[2, w] = partial(w, other).astype(BF16)
            go(w, cs.at[2, w], cr.at[2, w], partner)
        for w in range(3):
            acc[w] = partial(w, mine)
        yield
        for w in range(3):
            come(w, cr.at[2, w])
        for j in range(Z):
            first(j)
        yield
        for j in range(Z):
            second(j)
        yield
        sides = [fx[:, pl.ds(pl.multiple_of(c * 8, 8), 8), :], None]
        for j in range(Z - 1):
            for index in range(2):
                come(27 + 2 * j + index, q2.at[j, index])
        remote(
            fx.at[:, pl.ds(pl.multiple_of(o * 8, 8), 8), :], fr.at[:, :, other],
            pair_send.at[1], pair_recv.at[1], partner,
        ).wait_recv()
        sides[1] = fr[:, :, other]
        for j in range(Z - 1):
            for index in range(2):
                packed = q2[j, index].astype(F32)
                sides[index] = sides[index] + jnp.concatenate([packed[:, :8], packed[:, 8:]], axis=2)
        scale = 1.0 / math.sqrt(BLOCK)
        fr[:, :, mine] = sides[0] * scale
        fr[:, :, other] = sides[1] * scale
        yield

    def combine(partial, phase, buf, sign):
        def go(w, index, source, target, peer):
            push(source, target, ar_send.at[phase, w, index], ar_recv.at[phase, w, index], peer)

        def come(w, index, ref):
            remote(ref, ref, ar_send.at[phase, w, index], ar_recv.at[phase, w, index], partner).wait_recv()

        def block(w, x_, side):
            return buf.at[w, rows(x_ * ROWS, ROWS), side]

        def own(w, z_):
            return buf.at[w, rows((x * Z + z_) * PIECE, PIECE), mine]

        for w in range(3):
            cs[phase, w] = partial(w, other).astype(BF16)
            go(w, 0, cs.at[phase, w], cr.at[phase, w], partner)
        for w in range(3):
            acc[w] = partial(w, mine)
        yield
        for w in range(3):
            come(w, 0, cr.at[phase, w])
            for step in (2, 1, 3):
                span = rows(lax.rem(x + step, X) * ROWS, ROWS)
                sx[phase, w, step - 1] = (
                    acc[w, span, :] + cr[phase, w, span, :].astype(F32)
                ).astype(BF16)
                go(w, step, sx.at[phase, w, step - 1], qx.at[phase, w, step - 1], x_by(step))
        yield
        for w in range(3):
            span = rows(x * ROWS, ROWS)
            result = acc[w, span, :] + cr[phase, w, span, :].astype(F32)
            for step in (1, 3, 2):
                come(w, step, qx.at[phase, w, step - 1])
                result = result + qx[phase, w, step - 1].astype(F32)
            xblk[w] = result
            sz[phase, w] = result.astype(BF16)
            for step in (4, 3, 5, 2, 6, 1, 7):
                target = lax.rem(z + step, Z)
                go(
                    w, 3 + step, sz.at[phase, w, rows(target * PIECE, PIECE), :],
                    qz.at[phase, w, step - 1], z_by(step),
                )
            yield
        for w in range(3):
            result = xblk[w, rows(z * PIECE, PIECE), :]
            for step in (1, 7, 2, 6, 3, 5, 4):
                come(w, 3 + step, qz.at[phase, w, step - 1])
                result = result + qz[phase, w, step - 1].astype(F32)
            piece[phase, w] = result
            buf[w, rows(chip * PIECE, PIECE), mine] = (sign * result).astype(BF16)
            for step in (4, 3, 5, 2, 6, 1, 7):
                go(w, 10 + step, own(w, z), own(w, z), z_by(step))
        yield
        for w in range(3):
            for step in (1, 7, 2, 6, 3, 5, 4):
                come(w, 10 + step, own(w, lax.rem(z + Z - step, Z)))
            for step in (2, 1, 3):
                go(w, 17 + step, block(w, x, mine), block(w, x, mine), x_by(step))
            go(w, 21, block(w, x, mine), block(w, x, mine), partner)
        yield

    def finish(w, phase, buf):
        for step in (1, 3, 2):
            ref = buf.at[w, rows(lax.rem(x + X - step, X) * ROWS, ROWS), mine]
            remote(
                ref, ref, ar_send.at[phase, w, 17 + step], ar_recv.at[phase, w, 17 + step], partner
            ).wait_recv()
            remote(
                ref, ref, ar_send.at[phase, w, 21 + step], ar_recv.at[phase, w, 21 + step], partner
            ).start()

    def follow(w, phase, buf):
        for step in (0, 1, 3, 2):
            ref = buf.at[w, rows(lax.rem(x + X - step, X) * ROWS, ROWS), other]
            remote(
                ref, ref, ar_send.at[phase, w, 21 + step], ar_recv.at[phase, w, 21 + step], partner
            ).wait_recv()

    def leave(w, phase, buf):
        for step in (1, 3, 2):
            ref = buf.at[w, rows(lax.rem(x + X - step, X) * ROWS, ROWS), mine]
            remote(
                ref, ref, ar_send.at[phase, w, 21 + step], ar_recv.at[phase, w, 21 + step], partner
            ).wait_send()

    def run(steps):
        for _ in steps:
            pass

    gather()
    for load in loads[3:]:
        load.wait()

    keys, values = k_ref[...], v_ref[...]
    gate_pre, up_pre = mm(keys, w0[0]), mm(keys, w0[1])
    back = -mt(values, w0[2])
    gk_s[...], uk_s[...], back_s[...] = gate_pre, up_pre, back
    sigma = sigmoid(gate_pre)
    active = gate_pre * sigma
    hidden = (active * up_pre).astype(BF16)
    slope = sigma * (1.0 + gate_pre * (1.0 - sigma))
    rg[0] = (back * up_pre * slope).astype(BF16)
    rg[1] = (back * active).astype(BF16)
    rg[2] = values
    hid_k[...] = hidden
    hidn_t[...] = turned(-hidden.astype(F32))
    lt[0, :, T:] = turned(keys)
    rf[2, T:] = values

    def fast_partial(w, side):
        left_t = hidn_t[...] if w == 2 else lt[0, :, T:]
        return mm(left_t, rg[w, :, side])

    def apply_forward(b, weights):
        queries = q_ref[b]
        pre, upper = mm(queries, weights[0]), mm(queries, weights[1])
        sq = sigmoid(pre)
        hidden_q = (pre * sq * upper).astype(BF16)
        output = mm(hidden_q, weights[2])
        gq_s[...], uq_s[...], oq[...] = pre, upper, output
        weighted = gain_ref[...] * up_ref[b].astype(F32)
        power = jnp.sum(output * output, axis=1, keepdims=True)
        dots = jnp.sum(weighted * output, axis=1, keepdims=True)
        lane = lax.broadcasted_iota(jnp.int32, (T, T), 1)
        both = jnp.where(lane == 0, jnp.broadcast_to(power, (T, T)), jnp.broadcast_to(dots, (T, T)))
        st[b] = both.T[:8]
        for step in range(1, HEADS):
            push(
                st.at[b], sr.at[b, step - 1], st_send.at[b, step - 1], st_recv.at[b, step - 1],
                y_to[step - 1],
            )
        return hidden_q

    def apply_backward(b, weights, right_refs):
        total = st[b]
        for step in range(1, HEADS):
            remote(
                st.at[b], sr.at[b, step - 1], st_send.at[b, step - 1], st_recv.at[b, step - 1],
                y_to[step - 1],
            ).wait_recv()
            total = total + sr[b, step - 1]
        mean = total * (1.0 / (HEADS * D))
        inverse = lax.rsqrt(mean[0:1] + rms_eps)
        ratio = inverse * inverse * inverse * mean[1:2]
        down = jnp.where(
            lax.broadcasted_iota(jnp.int32, (T, T), 0) == 0,
            jnp.broadcast_to(inverse, (T, T)),
            jnp.broadcast_to(ratio, (T, T)),
        ).T
        weighted = gain_ref[...] * up_ref[b].astype(F32)
        d_output = (down[:, 0:1] * weighted - oq[...] * down[:, 1:2]).astype(BF16)
        back_q = mt(d_output, weights[2])
        pre, upper = gq_s[...], uq_s[...]
        sq = sigmoid(pre)
        right_refs[0][...] = (back_q * upper * (sq * (1.0 + pre * (1.0 - sq)))).astype(BF16)
        right_refs[1][...] = (back_q * pre * sq).astype(BF16)
        right_refs[2][...] = d_output

    def query_grad(b, weights, right_refs):
        gq_out[b] = (
            mt(right_refs[0][...], weights[0]) + mt(right_refs[1][...], weights[1])
        ).astype(BF16)

    first_refs = [rf.at[w, pl.ds(0, T), :] for w in range(3)]
    old = len(sent)
    steps = combine(fast_partial, 0, gh, 1.0)
    next(steps)
    next(steps)
    hidden_q = apply_forward(0, w0)
    lt[0, :, :T] = turned(q_ref[0])
    lt[1, :, :T] = turned(hidden_q)
    q1_t[...] = turned(q_ref[1])
    drain(old)
    next(steps)
    apply_backward(0, w0, first_refs)
    run(steps)
    finish(0, 0, gh)

    def schulz(w, carry):
        follow(w, 0, gh)
        fast = gh[w]
        fast32 = fast.astype(F32)
        power = jnp.sum(jnp.sum(fast32 * fast32, axis=1, keepdims=True), axis=0, keepdims=True)
        root = jnp.sqrt(power)
        norm = root + fro_eps
        inv = 1.0 / norm
        norms[w, 0:8] = jnp.broadcast_to(root, (8, 128))
        norms[w, 8:16] = jnp.broadcast_to(norm, (8, 128))
        gram = (mt(fast, fast) * (inv * inv)).astype(BF16)
        a0[w] = gram
        blend = (cube_coef * gram.astype(F32) + fifth_coef * mm(gram, gram)).astype(BF16)
        b0[w] = blend
        iterate = (inv * (lin_coef * gh[w].astype(F32) + mm(blend, gh[w]))).astype(BF16)
        x1[w] = iterate

        @pl.when(w < 2)
        def _():
            finish(w + 1, 0, gh)

        gram = mt(x1[w], x1[w]).astype(BF16)
        a1[w] = gram
        blend = (cube_coef * gram.astype(F32) + fifth_coef * mm(gram, gram)).astype(BF16)
        b1[w] = blend
        final = (lin_coef * x1[w].astype(F32) + mm(blend, x1[w])).astype(BF16)
        w1[w] = (w0[w].astype(F32) - final.astype(F32)).astype(BF16)
        return carry

    lax.fori_loop(0, 3, schulz, 0)

    hidden_q = apply_forward(1, w1)
    hq1_t[...] = turned(hidden_q)
    second_refs = [r1.at[w] for w in range(3)]
    apply_backward(1, w1, second_refs)

    def second_partial(w, side):
        left_t = hq1_t[...] if w == 2 else q1_t[...]
        return mm(left_t, r1[w, :, side])

    old = len(sent)
    steps = combine(second_partial, 1, pt, -1.0)
    next(steps)
    next(steps)
    query_grad(1, w1, second_refs)
    query_grad(0, w0, first_refs)
    drain(old)
    for w in range(3):
        leave(w, 0, gh)
    run(steps)
    finish(0, 1, pt)

    def schulz_back(w, carry):
        follow(w, 1, pt)
        root, norm = norms[w, 0:1, 0:1], norms[w, 8:9, 0:1]
        inv = 1.0 / norm

        def sweep(pair, gram, both, scale):
            cross = mt(pair[w, low], pair[w, high])
            cross = cross + cross.T
            if scale is not None:
                cross = cross * scale
            symmetric = cross.astype(BF16)
            bent = mm(symmetric, gram)
            bent = bent + bent.T
            mixed = cube_coef * symmetric.astype(F32) + fifth_coef * bent
            if scale is not None:
                mixed = mixed * scale
            both[w, :, high] = mixed.astype(BF16)
            return (lin_coef * pair[w, low].astype(F32) + mm(both[w], pair[w])).astype(BF16)

        yx0[w, low] = sweep(yx1, a1[w], be1, None)

        @pl.when(w < 2)
        def _():
            finish(w + 1, 1, pt)

        bottom = sweep(yx0, a0[w], be0, inv).astype(F32)
        fast = gh[w].astype(F32)
        inner = jnp.sum(jnp.sum(bottom * fast, axis=1, keepdims=True), axis=0, keepdims=True)
        cc[w] = (bottom * inv - fast * (inner / (norm * norm * root))).astype(BF16)
        return carry

    lax.fori_loop(0, 3, schulz_back, 0)

    keys, values = k_ref[...], v_ref[...]
    along_gate, along_up = mm(keys, cc[0]), mm(keys, cc[1])
    along_hidden = -mt(values, cc[2])
    gate_pre, up_pre, back = gk_s[...], uk_s[...], back_s[...]
    sigma = sigmoid(gate_pre)
    active = gate_pre * sigma
    slope = sigma * (1.0 + gate_pre * (1.0 - sigma))
    curve = sigma * (1.0 - sigma) * (2.0 + gate_pre * (1.0 - 2.0 * sigma))
    d_back = (along_gate * up_pre * slope + along_up * active).astype(BF16)
    rf[1, T:] = (along_gate * back * slope + along_hidden * active).astype(BF16)
    rf[0, T:] = (
        along_gate * back * up_pre * curve + along_up * back * slope + along_hidden * up_pre * slope
    ).astype(BF16)
    lt[1, :, T:] = turned(-d_back.astype(F32))
    r1[2] = d_back

    def last_partial(w, side):
        return mm(lt[w // 2], rf[w, :, side])

    old = len(sent)
    steps = reduce(last_partial)
    next(steps)
    next(steps)
    gk_out[...] = (
        mt(rg[0], cc[0]) + mt(rg[1], cc[1]) + mt(rf[0, T:], w0[0]) + mt(rf[1, T:], w0[1])
    ).astype(BF16)
    gv_out[...] = (-mm(hid_k[...], cc[2]) - mm(r1[2], w0[2])).astype(BF16)
    drain(old)
    for w in range(3):
        leave(w, 1, pt)
    next(steps)
    drain(3 + 3 * Z)
    run(steps)

    for w, out in enumerate((gg_out, gu_out, gd_out)):
        out[0] = fr[w]
    drain(len(sent))


def hand_on(*refs):
    copies = [
        pltpu.make_async_copy(refs[i], refs[6 + i], refs[12].at[i]) for i in range(6)
    ]
    for copy in copies:
        copy.start()
    for copy in copies:
        copy.wait()


def per_device(queries, keys, values, upstream, out_gain, gate_weight, up_weight, down_weight):
    vmem = pl.BlockSpec(memory_space=pltpu.VMEM)
    hbm = pl.BlockSpec(memory_space=pl.ANY)
    square = pltpu.VMEM((3, D, D), BF16)
    wide = pltpu.VMEM((T, D), F32)
    dma = pltpu.SemaphoreType.DMA
    scratch = [
        pltpu.VMEM((2, T, D), BF16), pltpu.VMEM((T, D), BF16), pltpu.VMEM((T, D), BF16),
        pltpu.VMEM((2, T, D), BF16), pltpu.VMEM((1, D), F32), pltpu.VMEM((3, 8, D), BF16), dma((8,)),
        pltpu.VMEM((3, X * Z, 2, 8, D), BF16),
    ] + [square] * 5 + [pltpu.VMEM((3, D, 2 * D), BF16)] * 2 + [pltpu.VMEM((3, 2 * D, D), BF16)] * 2 + [
        wide, wide, wide, pltpu.VMEM((T, D), BF16), pltpu.VMEM((D, T), BF16),
        pltpu.VMEM((3, T, D), BF16),
        pltpu.VMEM((D, T), BF16), pltpu.VMEM((D, T), BF16), pltpu.VMEM((3, T, D), BF16),
        pltpu.VMEM((2, D, 2 * T), BF16), pltpu.VMEM((3, 2 * T, D), BF16),
        wide, wide, wide, pltpu.VMEM((2, 8, 128), F32), pltpu.VMEM((2, 3, 8, 128), F32),
        pltpu.VMEM((3, 3, D, HALF), BF16), pltpu.VMEM((3, 3, D, HALF), BF16),
        pltpu.VMEM((3, D, HALF), F32),
    ] + [pltpu.VMEM((Z, 3, 3, PIECE, HALF), BF16)] * 2 + [pltpu.VMEM((Z - 1, 2, 3, PIECE, 128), BF16)] * 2 + [
        pltpu.VMEM((3, PIECE, HALF), F32),
        pltpu.VMEM((2, 3, 3, ROWS, HALF), BF16), pltpu.VMEM((2, 3, 3, ROWS, HALF), BF16),
        pltpu.VMEM((2, 3, ROWS, HALF), BF16), pltpu.VMEM((2, 3, Z - 1, PIECE, HALF), BF16),
        pltpu.VMEM((3, ROWS, HALF), F32),
        pltpu.VMEM((2, 3, PIECE, HALF), F32), pltpu.VMEM((3, 16, 128), F32),
        pltpu.VMEM((3, PIECE, HALF), F32), pltpu.VMEM((3, 8, D), F32),
        dma((35,)), dma((35,)), dma((41,)), dma((41,)), dma((2, 3, 25)), dma((2, 3, 25)),
        dma((2, 3)), dma((2, 3)), dma((2,)), dma((2,)),
    ]
    grad = jax.ShapeDtypeStruct((1, 8, D), F32)
    shapes = (
        jax.ShapeDtypeStruct((2, T, D), BF16), jax.ShapeDtypeStruct((T, D), BF16),
        jax.ShapeDtypeStruct((T, D), BF16), grad, grad, grad,
    )
    outs = pl.pallas_call(
        kernel,
        out_shape=tuple(pltpu.VMEM(shape.shape, shape.dtype) for shape in shapes),
        in_specs=[hbm] * 8,
        out_specs=[vmem] * 6,
        scratch_shapes=scratch,
        compiler_params=pltpu.CompilerParams(
            collective_id=0, has_side_effects=True, vmem_limit_bytes=60 * 1024 * 1024
        ),
    )(queries, keys, values, upstream, out_gain[None], gate_weight, up_weight, down_weight)
    return pl.pallas_call(
        hand_on, out_shape=shapes, in_specs=[vmem] * 6, out_specs=[hbm] * 6,
        scratch_shapes=[dma((6,))],
    )(*[pltpu.with_memory_space_constraint(out, pltpu.VMEM) for out in outs])


def solution(mesh):
    in_specs = (
        P(None, "tok", "head"),
        P("tok", "head"),
        P("tok", "head"),
        P(None, "tok", "head"),
        P("head"),
        P("head", "tok", None),
        P("head", "tok", None),
        P("head", "tok", None),
    )
    out_specs = (
        P(None, "tok", "head"),
        P("tok", "head"),
        P("tok", "head"),
        P("head", "tok", None),
        P("head", "tok", None),
        P("head", "tok", None),
    )
    return jax.shard_map(
        per_device, mesh=mesh, in_specs=in_specs, out_specs=out_specs, check_vma=False
    )
```

```python
import math

import jax
import jax.numpy as jnp
from jax import lax
from jax.experimental import pallas as pl
from jax.experimental.pallas import tpu as pltpu
from jax.sharding import PartitionSpec as P

lin_coef = 3.4445
cube_coef = -4.775
fifth_coef = 2.0315
rms_eps = 1e-06
fro_eps = 1e-07

X, Z, HEADS = 4, 8, 4
D = 512
BLOCK = 8192
T = 128
HALF = 256
PIECE = 16
ROWS = 128
F32, BF16 = jnp.float32, jnp.bfloat16
MESH = pl.DeviceIdType.MESH


def mm(a, b):
    return jnp.dot(a, b, preferred_element_type=F32)


def mt(a, b):
    return lax.dot_general(a, b, (((1,), (1,)), ((), ())), preferred_element_type=F32)


def sigmoid(v):
    return 1.0 / (1.0 + jnp.exp(-v))


def turned(v):
    return v.astype(F32).T.astype(BF16)


def kernel(
    q_hbm, k_hbm, v_hbm, up_hbm, gain_hbm, g_rows, u_rows, d_rows,
    gq_out, gk_out, gv_out, gg_out, gu_out, gd_out,
    q_ref, k_ref, v_ref, up_ref, gain_ref, wr, in_sem,
    wq, w0, w1, a0, a1, cc, be0, be1, yx0, yx1,
    gk_s, uk_s, back_s, hid_k, hidn_t, rg,
    q1_t, hq1_t, r1, lt, rf,
    oq, gq_s, uq_s, st, sr,
    cs, cr, acc, s1, q1, s2, q2, s2f, sx, qx, sz, qz, xblk,
    piece, norms, fx, fr,
    ag_send, ag_recv, rs_send, rs_recv, ar_send, ar_recv, st_send, st_recv, pair_send, pair_recv,
):
    low, high = pl.ds(0, D), pl.ds(D, D)
    gh, pt, x1 = yx0.at[:, high, :], yx1.at[:, low, :], yx1.at[:, high, :]
    b0, b1 = be0.at[:, :, low], be1.at[:, :, low]
    tok = lax.axis_index("tok")
    y = lax.axis_index("head")
    c = lax.rem(tok, 2)
    o = 1 - c
    chip = lax.div(tok, 2)
    z = lax.rem(chip, Z)
    x = lax.div(chip, Z)

    def device(x_, z_, c_):
        return ((x_ * Z + z_) * 2 + c_, y)

    partner = device(x, z, o)

    def x_by(step):
        return device(lax.rem(x + step, X), z, c)

    def z_by(step, core=c):
        return device(x, lax.rem(z + step + Z, Z), core)

    y_to = [(tok, lax.rem(y + step, HEADS)) for step in range(1, HEADS)]
    mine = pl.ds(pl.multiple_of(c * HALF, HALF), HALF)
    other = pl.ds(pl.multiple_of(o * HALF, HALF), HALF)

    def rows(start, size):
        return pl.ds(pl.multiple_of(start, 16), size)

    loads = [
        pltpu.make_async_copy(source, target, in_sem.at[i])
        for i, (source, target) in enumerate(
            (
                (g_rows.at[0], wr.at[0]), (u_rows.at[0], wr.at[1]), (d_rows.at[0], wr.at[2]),
                (k_hbm, k_ref), (v_hbm, v_ref), (q_hbm, q_ref), (up_hbm, up_ref),
                (gain_hbm, gain_ref),
            )
        )
    ]
    barrier = pltpu.get_barrier_semaphore()
    peers = [partner] + [x_by(step) for step in range(1, X)] + y_to
    for step in range(1, Z):
        peers += [z_by(step), z_by(step, o)]
    for peer in peers:
        pl.semaphore_signal(barrier, inc=1, device_id=peer, device_id_type=MESH)
    for load in loads:
        load.start()
    for w in range(3):
        loads[w].wait()
    pl.semaphore_wait(barrier, len(peers))

    sent = []

    def remote(source, target, send, recv, peer):
        return pltpu.make_async_remote_copy(
            src_ref=source, dst_ref=target, send_sem=send, recv_sem=recv,
            device_id=peer, device_id_type=MESH,
        )

    def drain(count):
        for copy in sent[:count]:
            copy.wait_send()
        del sent[:count]

    def push(*args):
        copy = remote(*args)
        copy.start()
        sent.append(copy)

    def gather():
        def go(index, source, target, peer):
            push(source, target, ag_send.at[index], ag_recv.at[index], peer)

        def come(index, ref):
            remote(ref, ref, ag_send.at[index], ag_recv.at[index], partner).wait_recv()

        def part(x_, z_):
            return wq.at[:, x_ * Z + lax.rem(z_ + Z, Z), c]

        def block(x_, core):
            return wq.at[:, pl.ds(x_ * Z, Z), core]

        offsets = (0, -1, 1, -2, 2, -3, 3, 4)

        def across(g):
            ref = part(x, z + offsets[g])
            for step in (1, 3, 2):
                go(6 + 3 * g + step, wr if g == 0 else ref, ref, x_by(step))

        for g in range(1, Z):
            go(g - 1, wr, part(x, z), z_by(-offsets[g]))
        across(0)
        wq[:, chip, c] = wr[...]
        for g in range(1, Z):
            come(g - 1, part(x, z + offsets[g]))
            across(g)
        go(31, block(x, c), block(x, c), partner)
        for step in (1, 3, 2):
            x_ = lax.rem(x + X - step, X)
            for g in range(Z):
                come(6 + 3 * g + step, part(x_, z + offsets[g]))
            go(31 + step, block(x_, c), block(x_, c), partner)
        for step in (0, 1, 3, 2):
            x_ = lax.rem(x + X - step, X)
            come(31 + step, block(x_, o))
            for w in range(3):
                whole = wq[w, pl.ds(x_ * Z, Z)].astype(F32)
                w0[w, rows(x_ * ROWS, ROWS), :] = whole.reshape(ROWS, D).astype(BF16)

    def reduce(partial):
        def go(index, source, target, peer):
            push(source, target, rs_send.at[index], rs_recv.at[index], peer)

        def come(index, ref):
            remote(ref, ref, rs_send.at[index], rs_recv.at[index], partner).wait_recv()

        offsets = (4, 3, -3, 2, -2, 1, -1, 0)

        def total(x_, j):
            span = rows((x_ * Z + lax.rem(z + offsets[j] + Z, Z)) * PIECE, PIECE)
            return acc[:, span, :] + cr[2, :, span, :].astype(F32)

        def first(j):
            for step in (2, 1, 3):
                s1[j, step - 1] = total(lax.rem(x + step, X), j).astype(BF16)
                go(2 + 3 * j + step, s1.at[j, step - 1], q1.at[j, step - 1], x_by(step))

        def second(j):
            result = total(x, j)
            for step in (1, 3, 2):
                come(2 + 3 * j + step, q1.at[j, step - 1])
                result = result + q1[j, step - 1].astype(F32)
            if j < Z - 1:
                s2f[...] = result
                for index, core in enumerate((c, o)):
                    rows8 = s2f[:, pl.ds(pl.multiple_of(core * 8, 8), 8), :]
                    s2[j, index] = jnp.concatenate(
                        [rows8[:, :, :128], rows8[:, :, 128:]], axis=1
                    ).astype(BF16)
                    go(27 + 2 * j + index, s2.at[j, index], q2.at[j, index], z_by(offsets[j], core))
            else:
                fx[...] = result + piece[1]
                push(
                    fx.at[:, pl.ds(pl.multiple_of(o * 8, 8), 8), :], fr.at[:, :, mine],
                    pair_send.at[1], pair_recv.at[1], partner,
                )

        for w in range(3):
            cs[2, w] = partial(w, other).astype(BF16)
            go(w, cs.at[2, w], cr.at[2, w], partner)
        for w in range(3):
            acc[w] = partial(w, mine)
        yield
        for w in range(3):
            come(w, cr.at[2, w])
        for j in range(Z):
            first(j)
        yield
        for j in range(Z):
            second(j)
        yield
        sides = [fx[:, pl.ds(pl.multiple_of(c * 8, 8), 8), :], None]
        for j in range(Z - 1):
            for index in range(2):
                come(27 + 2 * j + index, q2.at[j, index])
        remote(
            fx.at[:, pl.ds(pl.multiple_of(o * 8, 8), 8), :], fr.at[:, :, other],
            pair_send.at[1], pair_recv.at[1], partner,
        ).wait_recv()
        sides[1] = fr[:, :, other]
        for j in range(Z - 1):
            for index in range(2):
                packed = q2[j, index].astype(F32)
                sides[index] = sides[index] + jnp.concatenate([packed[:, :8], packed[:, 8:]], axis=2)
        scale = 1.0 / math.sqrt(BLOCK)
        fr[:, :, mine] = sides[0] * scale
        fr[:, :, other] = sides[1] * scale
        yield

    def combine(partial, phase, buf, sign):
        def go(w, index, source, target, peer):
            push(source, target, ar_send.at[phase, w, index], ar_recv.at[phase, w, index], peer)

        def come(w, index, ref):
            remote(ref, ref, ar_send.at[phase, w, index], ar_recv.at[phase, w, index], partner).wait_recv()

        def block(w, x_, side):
            return buf.at[w, rows(x_ * ROWS, ROWS), side]

        def own(w, z_):
            return buf.at[w, rows((x * Z + z_) * PIECE, PIECE), mine]

        for w in range(3):
            cs[phase, w] = partial(w, other).astype(BF16)
            go(w, 0, cs.at[phase, w], cr.at[phase, w], partner)
        for w in range(3):
            acc[w] = partial(w, mine)
        yield
        for w in range(3):
            come(w, 0, cr.at[phase, w])
            for step in (2, 1, 3):
                span = rows(lax.rem(x + step, X) * ROWS, ROWS)
                sx[phase, w, step - 1] = (
                    acc[w, span, :] + cr[phase, w, span, :].astype(F32)
                ).astype(BF16)
                go(w, step, sx.at[phase, w, step - 1], qx.at[phase, w, step - 1], x_by(step))
        yield
        for w in range(3):
            span = rows(x * ROWS, ROWS)
            result = acc[w, span, :] + cr[phase, w, span, :].astype(F32)
            for step in (1, 3, 2):
                come(w, step, qx.at[phase, w, step - 1])
                result = result + qx[phase, w, step - 1].astype(F32)
            xblk[w] = result
            sz[phase, w] = result.astype(BF16)
            for step in (4, 3, 5, 2, 6, 1, 7):
                target = lax.rem(z + step, Z)
                go(
                    w, 3 + step, sz.at[phase, w, rows(target * PIECE, PIECE), :],
                    qz.at[phase, w, step - 1], z_by(step),
                )
            yield
        for w in range(3):
            result = xblk[w, rows(z * PIECE, PIECE), :]
            for step in (1, 7, 2, 6, 3, 5, 4):
                come(w, 3 + step, qz.at[phase, w, step - 1])
                result = result + qz[phase, w, step - 1].astype(F32)
            piece[phase, w] = result
            buf[w, rows(chip * PIECE, PIECE), mine] = (sign * result).astype(BF16)
            for step in (4, 3, 5, 2, 6, 1, 7):
                go(w, 10 + step, own(w, z), own(w, z), z_by(step))
        yield
        for w in range(3):
            for step in (1, 7, 2, 6, 3, 5, 4):
                come(w, 10 + step, own(w, lax.rem(z + Z - step, Z)))
            for step in (2, 1, 3):
                go(w, 17 + step, block(w, x, mine), block(w, x, mine), x_by(step))
            go(w, 21, block(w, x, mine), block(w, x, mine), partner)
        yield

    def finish(w, phase, buf):
        for step in (1, 3, 2):
            ref = buf.at[w, rows(lax.rem(x + X - step, X) * ROWS, ROWS), mine]
            remote(
                ref, ref, ar_send.at[phase, w, 17 + step], ar_recv.at[phase, w, 17 + step], partner
            ).wait_recv()
            remote(
                ref, ref, ar_send.at[phase, w, 21 + step], ar_recv.at[phase, w, 21 + step], partner
            ).start()

    def follow(w, phase, buf):
        for step in (0, 1, 3, 2):
            ref = buf.at[w, rows(lax.rem(x + X - step, X) * ROWS, ROWS), other]
            remote(
                ref, ref, ar_send.at[phase, w, 21 + step], ar_recv.at[phase, w, 21 + step], partner
            ).wait_recv()

    def leave(w, phase, buf):
        for step in (1, 3, 2):
            ref = buf.at[w, rows(lax.rem(x + X - step, X) * ROWS, ROWS), mine]
            remote(
                ref, ref, ar_send.at[phase, w, 21 + step], ar_recv.at[phase, w, 21 + step], partner
            ).wait_send()

    def run(steps):
        for _ in steps:
            pass

    gather()
    for load in loads[3:]:
        load.wait()

    keys, values = k_ref[...], v_ref[...]
    gate_pre, up_pre = mm(keys, w0[0]), mm(keys, w0[1])
    back = -mt(values, w0[2])
    gk_s[...], uk_s[...], back_s[...] = gate_pre, up_pre, back
    sigma = sigmoid(gate_pre)
    active = gate_pre * sigma
    hidden = (active * up_pre).astype(BF16)
    slope = sigma * (1.0 + gate_pre * (1.0 - sigma))
    rg[0] = (back * up_pre * slope).astype(BF16)
    rg[1] = (back * active).astype(BF16)
    rg[2] = values
    hid_k[...] = hidden
    hidn_t[...] = turned(-hidden.astype(F32))
    lt[0, :, T:] = turned(keys)
    rf[2, T:] = values

    def fast_partial(w, side):
        left_t = hidn_t[...] if w == 2 else lt[0, :, T:]
        return mm(left_t, rg[w, :, side])

    def apply_forward(b, weights):
        queries = q_ref[b]
        pre, upper = mm(queries, weights[0]), mm(queries, weights[1])
        sq = sigmoid(pre)
        hidden_q = (pre * sq * upper).astype(BF16)
        output = mm(hidden_q, weights[2])
        gq_s[...], uq_s[...], oq[...] = pre, upper, output
        weighted = gain_ref[...] * up_ref[b].astype(F32)
        power = jnp.sum(output * output, axis=1, keepdims=True)
        dots = jnp.sum(weighted * output, axis=1, keepdims=True)
        lane = lax.broadcasted_iota(jnp.int32, (T, T), 1)
        both = jnp.where(lane == 0, jnp.broadcast_to(power, (T, T)), jnp.broadcast_to(dots, (T, T)))
        st[b] = both.T[:8]
        for step in range(1, HEADS):
            push(
                st.at[b], sr.at[b, step - 1], st_send.at[b, step - 1], st_recv.at[b, step - 1],
                y_to[step - 1],
            )
        return hidden_q

    def apply_backward(b, weights, right_refs):
        total = st[b]
        for step in range(1, HEADS):
            remote(
                st.at[b], sr.at[b, step - 1], st_send.at[b, step - 1], st_recv.at[b, step - 1],
                y_to[step - 1],
            ).wait_recv()
            total = total + sr[b, step - 1]
        mean = total * (1.0 / (HEADS * D))
        inverse = lax.rsqrt(mean[0:1] + rms_eps)
        ratio = inverse * inverse * inverse * mean[1:2]
        down = jnp.where(
            lax.broadcasted_iota(jnp.int32, (T, T), 0) == 0,
            jnp.broadcast_to(inverse, (T, T)),
            jnp.broadcast_to(ratio, (T, T)),
        ).T
        weighted = gain_ref[...] * up_ref[b].astype(F32)
        d_output = (down[:, 0:1] * weighted - oq[...] * down[:, 1:2]).astype(BF16)
        back_q = mt(d_output, weights[2])
        pre, upper = gq_s[...], uq_s[...]
        sq = sigmoid(pre)
        right_refs[0][...] = (back_q * upper * (sq * (1.0 + pre * (1.0 - sq)))).astype(BF16)
        right_refs[1][...] = (back_q * pre * sq).astype(BF16)
        right_refs[2][...] = d_output

    def query_grad(b, weights, right_refs):
        gq_out[b] = (
            mt(right_refs[0][...], weights[0]) + mt(right_refs[1][...], weights[1])
        ).astype(BF16)

    first_refs = [rf.at[w, pl.ds(0, T), :] for w in range(3)]
    old = len(sent)
    steps = combine(fast_partial, 0, gh, 1.0)
    next(steps)
    next(steps)
    hidden_q = apply_forward(0, w0)
    lt[0, :, :T] = turned(q_ref[0])
    lt[1, :, :T] = turned(hidden_q)
    q1_t[...] = turned(q_ref[1])
    drain(old)
    next(steps)
    apply_backward(0, w0, first_refs)
    run(steps)
    finish(0, 0, gh)

    def schulz(w, carry):
        follow(w, 0, gh)
        fast = gh[w]
        fast32 = fast.astype(F32)
        power = jnp.sum(jnp.sum(fast32 * fast32, axis=1, keepdims=True), axis=0, keepdims=True)
        root = jnp.sqrt(power)
        norm = root + fro_eps
        inv = 1.0 / norm
        norms[w, 0:8] = jnp.broadcast_to(root, (8, 128))
        norms[w, 8:16] = jnp.broadcast_to(norm, (8, 128))
        gram = (mt(fast, fast) * (inv * inv)).astype(BF16)
        a0[w] = gram
        blend = (cube_coef * gram.astype(F32) + fifth_coef * mm(gram, gram)).astype(BF16)
        b0[w] = blend
        iterate = (inv * (lin_coef * gh[w].astype(F32) + mm(blend, gh[w]))).astype(BF16)
        x1[w] = iterate

        @pl.when(w < 2)
        def _():
            finish(w + 1, 0, gh)

        gram = mt(x1[w], x1[w]).astype(BF16)
        a1[w] = gram
        blend = (cube_coef * gram.astype(F32) + fifth_coef * mm(gram, gram)).astype(BF16)
        b1[w] = blend
        final = (lin_coef * x1[w].astype(F32) + mm(blend, x1[w])).astype(BF16)
        w1[w] = (w0[w].astype(F32) - final.astype(F32)).astype(BF16)
        return carry

    lax.fori_loop(0, 3, schulz, 0)

    hidden_q = apply_forward(1, w1)
    hq1_t[...] = turned(hidden_q)
    second_refs = [r1.at[w] for w in range(3)]
    apply_backward(1, w1, second_refs)

    def second_partial(w, side):
        left_t = hq1_t[...] if w == 2 else q1_t[...]
        return mm(left_t, r1[w, :, side])

    old = len(sent)
    steps = combine(second_partial, 1, pt, -1.0)
    next(steps)
    next(steps)
    query_grad(1, w1, second_refs)
    query_grad(0, w0, first_refs)
    gate_pre, up_pre, back = gk_s[...], uk_s[...], back_s[...]
    sigma = sigmoid(gate_pre)
    slope = sigma * (1.0 + gate_pre * (1.0 - sigma))
    curve = sigma * (1.0 - sigma) * (2.0 + gate_pre * (1.0 - 2.0 * sigma))
    oq[...] = gate_pre * sigma
    gq_s[...] = back * slope
    uq_s[...] = back * up_pre * curve
    uk_s[...] = up_pre * slope
    drain(old)
    for w in range(3):
        leave(w, 0, gh)
    run(steps)
    finish(0, 1, pt)

    def schulz_back(w, carry):
        follow(w, 1, pt)
        root, norm = norms[w, 0:1, 0:1], norms[w, 8:9, 0:1]
        inv = 1.0 / norm

        def sweep(pair, gram, both, scale):
            cross = mt(pair[w, low], pair[w, high])
            cross = cross + cross.T
            if scale is not None:
                cross = cross * scale
            symmetric = cross.astype(BF16)
            bent = mm(symmetric, gram)
            bent = bent + bent.T
            mixed = cube_coef * symmetric.astype(F32) + fifth_coef * bent
            if scale is not None:
                mixed = mixed * scale
            both[w, :, high] = mixed.astype(BF16)
            return (lin_coef * pair[w, low].astype(F32) + mm(both[w], pair[w])).astype(BF16)

        yx0[w, low] = sweep(yx1, a1[w], be1, None)

        @pl.when(w < 2)
        def _():
            finish(w + 1, 1, pt)

        bottom = sweep(yx0, a0[w], be0, inv).astype(F32)
        fast = gh[w].astype(F32)
        inner = jnp.sum(jnp.sum(bottom * fast, axis=1, keepdims=True), axis=0, keepdims=True)
        cc[w] = (bottom * inv - fast * (inner / (norm * norm * root))).astype(BF16)
        return carry

    lax.fori_loop(0, 3, schulz_back, 0)

    keys, values = k_ref[...], v_ref[...]
    along_gate, along_up = mm(keys, cc[0]), mm(keys, cc[1])
    along_hidden = -mt(values, cc[2])
    d_back = (along_gate * uk_s[...] + along_up * oq[...]).astype(BF16)
    rf[1, T:] = (along_gate * gq_s[...] + along_hidden * oq[...]).astype(BF16)
    rf[0, T:] = (along_gate * uq_s[...] + along_up * gq_s[...] + along_hidden * uk_s[...]).astype(BF16)
    lt[1, :, T:] = turned(-d_back.astype(F32))
    r1[2] = d_back

    def last_partial(w, side):
        return mm(lt[w // 2], rf[w, :, side])

    old = len(sent)
    steps = reduce(last_partial)
    next(steps)
    next(steps)
    gk_out[...] = (
        mt(rg[0], cc[0]) + mt(rg[1], cc[1]) + mt(rf[0, T:], w0[0]) + mt(rf[1, T:], w0[1])
    ).astype(BF16)
    gv_out[...] = (-mm(hid_k[...], cc[2]) - mm(r1[2], w0[2])).astype(BF16)
    drain(old)
    for w in range(3):
        leave(w, 1, pt)
    next(steps)
    drain(3 + 3 * Z)
    run(steps)

    for w, out in enumerate((gg_out, gu_out, gd_out)):
        out[0] = fr[w]
    drain(len(sent))


def hand_on(*refs):
    copies = [
        pltpu.make_async_copy(refs[i], refs[6 + i], refs[12].at[i]) for i in range(6)
    ]
    for copy in copies:
        copy.start()
    for copy in copies:
        copy.wait()


def per_device(queries, keys, values, upstream, out_gain, gate_weight, up_weight, down_weight):
    vmem = pl.BlockSpec(memory_space=pltpu.VMEM)
    hbm = pl.BlockSpec(memory_space=pl.ANY)
    square = pltpu.VMEM((3, D, D), BF16)
    wide = pltpu.VMEM((T, D), F32)
    dma = pltpu.SemaphoreType.DMA
    scratch = [
        pltpu.VMEM((2, T, D), BF16), pltpu.VMEM((T, D), BF16), pltpu.VMEM((T, D), BF16),
        pltpu.VMEM((2, T, D), BF16), pltpu.VMEM((1, D), F32), pltpu.VMEM((3, 8, D), BF16), dma((8,)),
        pltpu.VMEM((3, X * Z, 2, 8, D), BF16),
    ] + [square] * 5 + [pltpu.VMEM((3, D, 2 * D), BF16)] * 2 + [pltpu.VMEM((3, 2 * D, D), BF16)] * 2 + [
        wide, wide, wide, pltpu.VMEM((T, D), BF16), pltpu.VMEM((D, T), BF16),
        pltpu.VMEM((3, T, D), BF16),
        pltpu.VMEM((D, T), BF16), pltpu.VMEM((D, T), BF16), pltpu.VMEM((3, T, D), BF16),
        pltpu.VMEM((2, D, 2 * T), BF16), pltpu.VMEM((3, 2 * T, D), BF16),
        wide, wide, wide, pltpu.VMEM((2, 8, 128), F32), pltpu.VMEM((2, 3, 8, 128), F32),
        pltpu.VMEM((3, 3, D, HALF), BF16), pltpu.VMEM((3, 3, D, HALF), BF16),
        pltpu.VMEM((3, D, HALF), F32),
    ] + [pltpu.VMEM((Z, 3, 3, PIECE, HALF), BF16)] * 2 + [pltpu.VMEM((Z - 1, 2, 3, PIECE, 128), BF16)] * 2 + [
        pltpu.VMEM((3, PIECE, HALF), F32),
        pltpu.VMEM((2, 3, 3, ROWS, HALF), BF16), pltpu.VMEM((2, 3, 3, ROWS, HALF), BF16),
        pltpu.VMEM((2, 3, ROWS, HALF), BF16), pltpu.VMEM((2, 3, Z - 1, PIECE, HALF), BF16),
        pltpu.VMEM((3, ROWS, HALF), F32),
        pltpu.VMEM((2, 3, PIECE, HALF), F32), pltpu.VMEM((3, 16, 128), F32),
        pltpu.VMEM((3, PIECE, HALF), F32), pltpu.VMEM((3, 8, D), F32),
        dma((35,)), dma((35,)), dma((41,)), dma((41,)), dma((2, 3, 25)), dma((2, 3, 25)),
        dma((2, 3)), dma((2, 3)), dma((2,)), dma((2,)),
    ]
    grad = jax.ShapeDtypeStruct((1, 8, D), F32)
    shapes = (
        jax.ShapeDtypeStruct((2, T, D), BF16), jax.ShapeDtypeStruct((T, D), BF16),
        jax.ShapeDtypeStruct((T, D), BF16), grad, grad, grad,
    )
    outs = pl.pallas_call(
        kernel,
        out_shape=tuple(pltpu.VMEM(shape.shape, shape.dtype) for shape in shapes),
        in_specs=[hbm] * 8,
        out_specs=[vmem] * 6,
        scratch_shapes=scratch,
        compiler_params=pltpu.CompilerParams(
            collective_id=0, has_side_effects=True, vmem_limit_bytes=60 * 1024 * 1024
        ),
    )(queries, keys, values, upstream, out_gain[None], gate_weight, up_weight, down_weight)
    return pl.pallas_call(
        hand_on, out_shape=shapes, in_specs=[vmem] * 6, out_specs=[hbm] * 6,
        scratch_shapes=[dma((6,))],
    )(*[pltpu.with_memory_space_constraint(out, pltpu.VMEM) for out in outs])


def solution(mesh):
    in_specs = (
        P(None, "tok", "head"),
        P("tok", "head"),
        P("tok", "head"),
        P(None, "tok", "head"),
        P("head"),
        P("head", "tok", None),
        P("head", "tok", None),
        P("head", "tok", None),
    )
    out_specs = (
        P(None, "tok", "head"),
        P("tok", "head"),
        P("tok", "head"),
        P("head", "tok", None),
        P("head", "tok", None),
        P("head", "tok", None),
    )
    return jax.shard_map(
        per_device, mesh=mesh, in_specs=in_specs, out_specs=out_specs, check_vma=False
    )
```
